512 devices in a mesh: seq: 64 (over z, x, core), head: 8 (over y).
Axes of the slice: x: 4, y: 8, z: 8, core: 2. Of those that a mesh axis runs over, the one named last changes fastest.
Arguments:
- queries: bfloat16 [32768, 3072], P('seq', 'head'), may hold values from -6 to 6
- key_vectors: bfloat16 [32768, 3072], P('seq', 'head'), may hold values from -6 to 6
- value_vectors: bfloat16 [32768, 3072], P('seq', 'head'), may hold values from -6 to 6
- doc_lengths: int32 [16], replicated, may hold values from 1 to 20480, 32768 in all
- norm_gain: float32 [3072], P('head'), may hold values from 0.1 to 1.9
- out_weight: bfloat16 [3072, 4096], P('head'), may hold values from -0.15625 to 0.15625
Outputs:
- layer_out: bfloat16 [32768, 4096], P('seq', 'head')
The draws below stay inside these ranges and needn't reach their ends.
Inputs may be any that keep to these rules, and one draw needn't show every extreme that they name: doc_lengths sum to 32768; the longest document has exactly 20480 tokens.
All inputs are finite; a program needn't handle non-finite values.
Results may differ from the reference program's by a relative error of at most 0.014.
Values may be sent and summed in bfloat16 or wider, within the bound.
A program may use at most 64 MiB of HBM per device.

```python
import math
import jax
import jax.numpy as jnp
import numpy as np
from jax import lax

D = 4096
DH = 128
HEADS = 24
TOK_DEV = 512
NDOC = 16
TOKENS = 32768
MOST = 20480
N_SEQ = 64
N_HEAD = 8


def with_spikes(entries, own_key, source, target, parts, factor):
    def block_of(dim):
        return (jnp.arange(entries.shape[dim]) // (entries.shape[dim] // parts)).reshape((-1,) + (1,) * (entries.ndim - 1 - dim))

    near = jax.random.permutation(own_key, parts)[block_of(target)]
    other_side = (block_of(target) + parts // 2) % parts
    return jnp.where((block_of(source) == near) | (block_of(source) == other_side), factor * entries, entries)


def block_levels(rng, dims, pieces, low, largest):
    loudness, own = 1.0, jax.random.fold_in(rng, 6)
    for dim, shards_of in pieces:
        draws = jnp.exp(jax.random.uniform(jax.random.fold_in(own, dim), (shards_of,), jnp.float32, low / len(pieces), largest / len(pieces)))
        loudness = loudness * jnp.repeat(draws, dims[dim] // shards_of).reshape([-1 if axis == dim else 1 for axis in range(len(dims))])
    return loudness


def split_up(count, total, most, skew):
    weights = [(1 << 20) // math.isqrt(rank ** skew) + 1 for rank in range(2, count + 1)]
    surplus, counts = total - most - (count - 1), [1] * (count - 1)
    while surplus > 0:
        free = [i for i in range(count - 1) if counts[i] < most]
        mass, budget = sum([weights[i] for i in free]), surplus
        for i in free:
            more = min(most - counts[i], max(1, budget * weights[i] // mass), surplus)
            counts[i] = counts[i] + more
            surplus = surplus - more
    return np.array([most] + counts)


def ragged_sizes(key, count, total, reach, slope):
    if count == 2:
        one = jax.random.randint(key, (), max(1, total - reach), min(reach, total - 1) + 1)
        return jnp.stack([one, total - one])
    lengths = jnp.asarray(split_up(count, total, reach, slope), jnp.int32)
    pairs = (count - 1) // 2
    source_of, sink = lengths[1:1 + 2 * pairs:2], lengths[2:2 + 2 * pairs:2]
    slack = jnp.minimum(source_of - 1, reach - sink)
    passed = jax.random.randint(jax.random.fold_in(key, 1), (pairs,), 0, 1 << 20) % (slack + 1)
    lengths = lengths.at[1:1 + 2 * pairs:2].set(source_of - passed).at[2:2 + 2 * pairs:2].set(sink + passed)
    return lengths[jax.random.permutation(jax.random.fold_in(key, 2), count)]


def scatter_about(rng, extent, width, reach, cuts=(), kind=jnp.bfloat16):
    entries = jax.random.normal(rng, extent, jnp.float32) * width
    if len(cuts) > 0:
        entries = block_levels(rng, extent, cuts, -0.22, 0.18) * entries
    return jnp.clip(entries, min=-reach, max=reach).astype(kind)


def bell_draw_with(key, shape, width, most, pieces, heavy, held_as=jnp.bfloat16):
    array = width * jax.random.normal(key, shape, jnp.float32)
    if pieces:
        array = array * block_levels(key, shape, pieces, -0.22, 0.18)
    return jnp.clip(with_spikes(array, jax.random.fold_in(key, 3), *heavy), -most, most).astype(held_as)


def setup_inputs(seed: int = 0) -> dict:
    key_of = jax.random.split(jax.random.key(seed), 7)
    queries = scatter_about(key_of[0], (TOKENS, HEADS * DH), 1.0, 6.0, ((0, 64), (1, 8)))
    key_vectors = scatter_about(key_of[1], (TOKENS, HEADS * DH), 1.0, 6.0, ((0, 64), (1, 8)))
    value_vectors = scatter_about(key_of[2], (TOKENS, HEADS * DH), 1.0, 6.0, ((0, 64), (1, 8)))
    doc_lengths = ragged_sizes(key_of[3], NDOC, TOKENS, MOST, 2).astype(jnp.int32)
    norm_gain = jnp.clip(1.0 + 0.18 * jax.random.normal(key_of[4], (HEADS * DH,), jnp.float32), 0.1, 1.9)
    out_weight = bell_draw_with(key_of[5], (HEADS * DH, D), (HEADS * DH) ** -0.5, 0.15625, ((0, 8),), (0, 1, 8, 2.0))
    return {"queries": queries, "key_vectors": key_vectors, "value_vectors": value_vectors, "doc_lengths": doc_lengths, "norm_gain": norm_gain, "out_weight": out_weight}


def reference(queries, key_vectors, value_vectors, doc_lengths, norm_gain, out_weight):
    head_count = queries.shape[1] // DH
    group_width = head_count // N_HEAD * DH
    doc_bounds = jnp.cumsum(doc_lengths).astype(jnp.int32)
    positions = jnp.arange(TOKENS, dtype=jnp.int32)
    before = doc_bounds[None, :] <= positions[:, None]
    segment = lax.optimization_barrier(jnp.sum(before.astype(jnp.int32), axis=1)).astype(jnp.int32)
    starts = lax.optimization_barrier(jnp.sum(jnp.where(before, doc_lengths[None, :], 0), axis=1)).astype(jnp.int32)
    block_shape = (N_SEQ, TOK_DEV, head_count, DH)
    block_items = (queries.reshape(block_shape), key_vectors.reshape(block_shape), value_vectors.reshape(block_shape), segment.reshape(N_SEQ, TOK_DEV), starts.reshape(N_SEQ, TOK_DEV), jnp.arange(N_SEQ, dtype=jnp.int32))
    gain_heads = norm_gain.reshape(head_count, DH).astype(jnp.float32)

    def advance(running, block_item):
        query_h, key_h, value_h, seg_block, start_block, block_index = block_item
        offset = block_index * TOK_DEV
        row_ids = jnp.arange(TOK_DEV, dtype=jnp.int32)
        allowed = (row_ids[None, :] <= row_ids[:, None]) & (seg_block[None, :] == seg_block[:, None])
        scores = jnp.einsum('thd,shd->hts', query_h.astype(jnp.float32), key_h.astype(jnp.float32))
        scores = lax.optimization_barrier(jnp.where(allowed[None], scores, 0.0).astype(jnp.bfloat16))
        within = jnp.einsum('hts,shd->thd', scores.astype(jnp.float32), value_h.astype(jnp.float32))
        last_rows = seg_block == seg_block[-1]
        key_last = jnp.where(last_rows[:, None, None], key_h, jnp.zeros_like(key_h))
        block_state = jnp.einsum('thd,the->hde', key_last.astype(jnp.float32), value_h.astype(jnp.float32))
        carried = lax.optimization_barrier(running.astype(jnp.bfloat16))
        cross_rows = (seg_block == seg_block[0]) & (start_block[0] < offset)
        query_cross = jnp.where(cross_rows[:, None, None], query_h, jnp.zeros_like(query_h))
        carried_term = jnp.einsum('thd,hde->the', query_cross.astype(jnp.float32), carried.astype(jnp.float32))
        mixture = within + carried_term
        square_mean = lax.optimization_barrier(jnp.mean(mixture * mixture, axis=-1, keepdims=True))
        normed = (mixture * lax.rsqrt(square_mean + 1e-06) * gain_heads).astype(jnp.bfloat16)
        normed = normed.reshape(TOK_DEV, head_count * DH)
        summed = jnp.zeros((TOK_DEV, D), jnp.float32)
        for member in range(N_HEAD):
            lower = member * group_width
            partial_value = jnp.dot(normed[:, lower:lower + group_width], out_weight[lower:lower + group_width], preferred_element_type=jnp.float32)
            partial_value = lax.optimization_barrier(partial_value.astype(jnp.bfloat16))
            summed = summed + partial_value.astype(jnp.float32)
        restart = start_block[-1] >= offset
        next_state = block_state + jnp.where(restart, jnp.zeros_like(running), running)
        return (next_state, summed.astype(jnp.bfloat16))
    initial = jnp.zeros((head_count, DH, DH), jnp.float32)
    final_state, outputs = lax.scan(advance, initial, block_items)
    return outputs.reshape(TOKENS, D)
```

```python
import functools

import jax
import jax.numpy as jnp
from jax import lax
from jax.experimental import pallas as pl
from jax.experimental.pallas import tpu as pltpu
from jax.sharding import PartitionSpec as P

DH = 128
ROW = 8
MESH = pl.DeviceIdType.MESH
F32 = jnp.float32
BF16 = jnp.bfloat16


def dot(a, b, dims=((1,), (0,))):
    return lax.dot_general(a, b, (dims, ((), ())), preferred_element_type=F32)


def layer_kernel(
    nz, row, ny,
    q_any, k_any, v_any, lens, gain, w_any, out_any,
    q_ref, k_ref, v_ref, s_loc, s_in, r_in, crow, c_out, c_in, lo_ref, within, norm_all, wcol, acc, out_v,
    load_sem, p1s, p1r, p2s, p2r, p3s, p3r, wys, wyr, wxs, wxr, wzs, wzr, wcs, wcr, ys, yr,
):
    tok, width = q_ref.shape
    heads = width // DH
    cols = out_v.shape[1]
    nx = row // 2
    yh, zh = ny // 2, nz // 2
    sl = width // row
    wr = width // nz
    xc = cols // nx
    seq, y = lax.axis_index("seq"), lax.axis_index("head")
    z, r = seq // row, seq % row
    x, c = r // 2, r % 2
    sends = []

    def remote(src, dst, ssem, rsem, target):
        return pltpu.make_async_remote_copy(
            src_ref=src, dst_ref=dst, send_sem=ssem, recv_sem=rsem,
            device_id=target, device_id_type=MESH)

    def send(*args):
        copy = remote(*args)
        copy.start()
        sends.append(copy)

    def row_dev(i):
        return (z * row + i, y)

    def z_dev(i):
        return (i * row + r, y)

    def y_dev(i):
        return (seq, i)

    barrier = pltpu.get_barrier_semaphore()
    peers = [row_dev((r + k) % row) for k in range(1, row)]
    peers += [z_dev((z + k) % nz) for k in range(1, nz)]
    peers += [y_dev((y + k) % ny) for k in range(1, ny)]
    for peer in peers:
        pl.semaphore_signal(barrier, inc=1, device_id=peer, device_id_type=MESH)

    loads = [
        pltpu.make_async_copy(k_any, k_ref, load_sem.at[0]),
        pltpu.make_async_copy(v_any, v_ref, load_sem.at[1]),
        pltpu.make_async_copy(q_any, q_ref, load_sem.at[2]),
        pltpu.make_async_copy(
            w_any.at[:, pl.ds(pl.multiple_of(y * cols, 128), cols)], wcol.at[0], load_sem.at[3]),
    ]
    for load in loads:
        load.start()

    bounds, total = [], jnp.int32(0)
    for d in range(lens.shape[0]):
        total = total + lens[d]
        bounds.append(total)

    def start_of(position):
        found = jnp.int32(0)
        for bound in bounds:
            found = jnp.where(bound <= position, bound, found)
        return found

    def flag(condition):
        return jnp.where(condition, jnp.float32(1), jnp.float32(0))

    offset = seq * tok
    lo_last = start_of(offset + (tok - 1)) - offset
    first = z * row
    row_start = [start_of((first + i) * tok) for i in range(row)]
    next_start = start_of((first + row) * tok)
    w_row_sum = [flag((first + j + 1) * tok > next_start) for j in range(row)]
    w_past = [flag(row_start[i] < first * tok) for i in range(row)]
    w_rows = [flag(((i + 1) * row * tok > row_start[0]) & (i < z)) for i in range(nz)]

    rows = lax.broadcasted_iota(jnp.int32, (tok, DH), 0)
    keep = flag(rows >= lo_last)
    loads[0].wait()
    loads[1].wait()
    for h in range(heads):
        hs = slice(h * DH, (h + 1) * DH)
        key = (k_ref[:, hs].astype(F32) * keep).astype(BF16)
        s_loc[hs, :] = dot(key, v_ref[:, hs], ((0,), (0,))).astype(BF16)

    pl.semaphore_wait(barrier, len(peers))

    def part(i):
        return pl.ds(pl.multiple_of(i * sl, 16), sl)

    for k in range(1, row):
        i = (r + k) % row
        send(s_loc.at[part(i)], s_in.at[r], p1s.at[k], p1r.at[k], row_dev(i))

    first_rel = 1 + (yh - 1) * c
    z_rows = pl.ds(pl.multiple_of(z * wr, 16), wr)
    x_cols = pl.ds(pl.multiple_of(x * xc, 128), xc)
    for i in range(yh):
        rel = first_rel + i
        plane = (y + ny - rel) % ny
        send(
            w_any.at[z_rows, pl.ds(pl.multiple_of(plane * cols + x * xc, 128), xc)],
            wcol.at[rel, z_rows, x_cols], wys.at[i], wyr.at[i], y_dev(plane))

    s_in[r] = s_loc[part(r), :]
    lo = jnp.zeros((tok, DH), jnp.int32) - offset
    for bound in bounds:
        lo = jnp.where(rows >= bound - offset, bound - offset, lo)
    lo_ref[...] = lo
    loads[2].wait()

    tb = tok // 2

    def attend(h):
        hs = slice(h * DH, (h + 1) * DH)
        for b in range(2):
            upto = (b + 1) * tb
            ts = slice(b * tb, upto)
            scores = dot(q_ref[ts, hs], k_ref[:upto, hs], ((1,), (1,)))
            t_ids = lax.broadcasted_iota(jnp.int32, (tb, upto), 0) + b * tb
            s_ids = lax.broadcasted_iota(jnp.int32, (tb, upto), 1)
            low = jnp.broadcast_to(lo_ref[ts, 0:1], (tb, upto))
            allowed = (s_ids <= t_ids) & (s_ids >= low)
            scores = jnp.where(allowed, scores, 0.0).astype(BF16)
            within[h, ts, :] = dot(scores, v_ref[:upto, hs])

    attend(0)

    for k in range(1, row):
        j = (r + row - k) % row
        remote(s_loc.at[part(j)], s_in.at[j], p1s.at[k], p1r.at[k], row_dev(j)).wait_recv()

    state = [s_in[j].astype(F32) for j in range(row)]
    row_sum = functools.reduce(jnp.add, [w_row_sum[j] * state[j] for j in range(row)])
    r_in[z] = row_sum.astype(BF16)
    for k in range(1, nz):
        send(r_in.at[z], r_in.at[z], p2s.at[k], p2r.at[k], z_dev((z + k) % nz))

    rels = pl.ds(first_rel, yh)
    for i in range(yh):
        rel = first_rel + i
        remote(
            w_any.at[z_rows, pl.ds(0, xc)], wcol.at[rel, z_rows, x_cols],
            wys.at[i], wyr.at[i], y_dev((y + rel) % ny)).wait_recv()
    for k in range(1, nx):
        block = wcol.at[rels, z_rows, x_cols]
        send(block, block, wxs.at[k], wxr.at[k], row_dev((x + k) % nx * 2 + c))

    for i in range(row):
        total = jnp.zeros((sl, DH), F32)
        for j in range(i):
            total = total + flag((first + j + 1) * tok > row_start[i]) * state[j]
        crow[i] = total
    attend(1)

    for k in range(1, nz):
        i = (z + nz - k) % nz
        remote(r_in.at[i], r_in.at[i], p2s.at[k], p2r.at[k], z_dev(i)).wait_recv()

    past = functools.reduce(jnp.add, [w_rows[i] * r_in[i].astype(F32) for i in range(nz)])
    for i in range(row):
        c_out[i] = (crow[i] + w_past[i] * past).astype(BF16)
    for k in range(1, row):
        i = (r + k) % row
        send(c_out.at[i], c_in.at[part(r)], p3s.at[k], p3r.at[k], row_dev(i))
    c_in[part(r), :] = c_out[r]

    attend(2)

    for k in range(1, nx):
        i = (x + nx - k) % nx
        block = wcol.at[rels, z_rows, pl.ds(pl.multiple_of(i * xc, 128), xc)]
        remote(block, block, wxs.at[k], wxr.at[k], row_dev(i * 2 + c)).wait_recv()

    def z_block(i, first, count):
        return wcol.at[pl.ds(first, count), pl.ds(pl.multiple_of(i * wr, 16), wr), :]

    def z_copy(way, d, starting):
        step = 1 if way == 0 else nz - 1
        away = d if starting else d + 1
        owner = (z + away * (nz - step)) % nz
        if d < zh - 1:
            block = z_block(owner, first_rel, yh)
        elif way == 0:
            block = z_block(owner, first_rel, yh // 2)
        else:
            block = z_block(owner, first_rel + yh // 2, yh - yh // 2)
        return block, block, wzs.at[way, d], wzr.at[way, d], z_dev((z + step) % nz)

    own_rels, twin_rels = 1 + yh * c, 1 + yh * (1 - c)
    twin = row_dev(x * 2 + (1 - c))

    def to_twin(i, n):
        block = z_block(i, own_rels, yh - 1)
        send(block, block, wcs.at[n], wcr.at[n], twin)

    def z_step(d):
        if d > 0:
            for way in range(2):
                remote(*z_copy(way, d - 1, False)).wait_recv()
        if d < zh:
            for way in range(2):
                send(*z_copy(way, d, True))
        if d == 0 or d == zh:
            to_twin((z + d) % nz, d)
        else:
            to_twin((z + d) % nz, d)
            to_twin((z + nz - d) % nz, nz - d)

    def twin_wait():
        for n in range(nz):
            block = z_block((z + n) % nz, twin_rels, yh - 1)
            remote(block, block, wcs.at[n], wcr.at[n], twin).wait_recv()

    z_step(0)

    for k in range(1, row):
        j = (r + row - k) % row
        remote(c_out.at[j], c_in.at[part(j)], p3s.at[k], p3r.at[k], row_dev(j)).wait_recv()

    def y_copy(way, d, h, starting):
        slot = (ny - d) % ny if way == 0 else d
        later = ny - d - 1 if way == 0 else d + 1
        ts = pl.ds(0, tok)
        if d == yh - 1:
            ts = pl.ds(way * tb, tb)
        src, dst = norm_all.at[slot, h, ts], norm_all.at[later, h, ts]
        to = (y + 1) % ny if way == 0 else (y + ny - 1) % ny
        return src, dst, ys.at[way, d, h], yr.at[way, d, h], y_dev(to)

    def y_send(d, h):
        for way in range(2):
            send(*y_copy(way, d, h, True))

    def y_wait(d, h, ways=(0, 1)):
        for way in ways:
            remote(*y_copy(way, d - 1, h, False)).wait_recv()

    for h in range(heads):
        hs = slice(h * DH, (h + 1) * DH)
        carried = c_in[hs, :]
        scale = gain[:, hs]
        for b in range(2):
            ts = slice(b * tb, (b + 1) * tb)
            term = dot(q_ref[ts, hs], carried)
            mixture = within[h, ts, :] + jnp.where(lo_ref[ts, :] < 0, term, 0.0)
            square_mean = jnp.mean(mixture * mixture, axis=-1, keepdims=True)
            norm_all[0, h, ts, :] = (mixture * lax.rsqrt(square_mean + 1e-06) * scale).astype(BF16)
        y_send(0, h)

    def project(rel, start=False):
        for b in range(2):
            ts = slice(b * tb, (b + 1) * tb)
            left = jnp.concatenate([norm_all[rel, h, ts, :] for h in range(heads)], axis=1)
            term = dot(left, wcol[rel])
            acc[ts, :] = term if start else acc[ts, :] + term

    def y_step(d, h):
        y_wait(d, h)
        y_send(d, h)

    loads[3].wait()
    project(0, True)
    z_left = list(range(1, zh + 1))
    n = 0
    for d in range(1, yh):
        if d == yh - 1:
            while z_left:
                z_step(z_left.pop(0))
            twin_wait()
            for e in range(1, d):
                project(e)
                project(ny - e)
        for h in range(heads):
            y_step(d, h)
            n += 1
            if n in (1, 3, 5, 6) and z_left:
                z_step(z_left.pop(0))
    project(yh - 1)
    project(yh + 1)
    for h in range(heads):
        hs = slice(h * DH, (h + 1) * DH)
        for way in range(2):
            ts = slice(way * tb, (way + 1) * tb)
            y_wait(yh, h, (way,))
            total = acc[ts, :] + dot(norm_all[yh, h, ts, :], wcol[yh, hs, :])
            if h < heads - 1:
                acc[ts, :] = total
            else:
                out_v[ts, :] = total.astype(BF16)
                load_sem_way = load_sem.at[way]
                pltpu.make_async_copy(out_v.at[ts], out_any.at[ts], load_sem_way).start()
    for copy in sends:
        copy.wait_send()
    for way in range(2):
        ts = slice(way * tb, (way + 1) * tb)
        pltpu.make_async_copy(out_v.at[ts], out_any.at[ts], load_sem.at[way]).wait()


def body(nz, row, ny, queries, key_vectors, value_vectors, doc_lengths, norm_gain, out_weight):
    tok, width = queries.shape
    heads = width // DH
    cols = out_weight.shape[1] // ny
    yh, zh = ny // 2, nz // 2
    sl = width // row
    dma = pltpu.SemaphoreType.DMA
    any_spec = pl.BlockSpec(memory_space=pl.ANY)
    return pl.pallas_call(
        functools.partial(layer_kernel, nz, row, ny),
        name="layer",
        out_shape=jax.ShapeDtypeStruct((tok, cols), BF16),
        in_specs=[
            any_spec, any_spec, any_spec,
            pl.BlockSpec(memory_space=pltpu.SMEM),
            pl.BlockSpec(memory_space=pltpu.VMEM),
            any_spec,
        ],
        out_specs=any_spec,
        scratch_shapes=[
            pltpu.VMEM((tok, width), BF16),
            pltpu.VMEM((tok, width), BF16),
            pltpu.VMEM((tok, width), BF16),
            pltpu.VMEM((width, DH), BF16),
            pltpu.VMEM((row, sl, DH), BF16),
            pltpu.VMEM((nz, sl, DH), BF16),
            pltpu.VMEM((row, sl, DH), F32),
            pltpu.VMEM((row, sl, DH), BF16),
            pltpu.VMEM((width, DH), BF16),
            pltpu.VMEM((tok, DH), jnp.int32),
            pltpu.VMEM((heads, tok, DH), F32),
            pltpu.VMEM((ny, heads, tok, DH), BF16),
            pltpu.VMEM((ny, width, cols), BF16),
            pltpu.VMEM((tok, cols), F32),
            pltpu.VMEM((tok, cols), BF16),
            dma((4,)),
            dma((row,)), dma((row,)),
            dma((nz,)), dma((nz,)),
            dma((row,)), dma((row,)),
            dma((yh,)), dma((yh,)),
            dma((row // 2,)), dma((row // 2,)),
            dma((2, zh)), dma((2, zh)),
            dma((nz,)), dma((nz,)),
            dma((2, yh, heads)), dma((2, yh, heads)),
        ],
        compiler_params=pltpu.CompilerParams(collective_id=0, has_side_effects=True),
    )(queries, key_vectors, value_vectors, doc_lengths, norm_gain.reshape(1, width), out_weight)


def solution(mesh, row=ROW):
    nz, ny = mesh.shape["seq"] // row, mesh.shape["head"]
    return jax.shard_map(
        functools.partial(body, nz, row, ny),
        mesh=mesh,
        in_specs=(
            P("seq", "head"),
            P("seq", "head"),
            P("seq", "head"),
            P(),
            P("head"),
            P("head", None),
        ),
        out_specs=P("seq", "head"),
        check_vma=False,
    )
```

```python
import functools

import jax
import jax.numpy as jnp
from jax import lax
from jax.experimental import pallas as pl
from jax.experimental.pallas import tpu as pltpu
from jax.sharding import PartitionSpec as P

DH = 128
ROW = 8
MESH = pl.DeviceIdType.MESH
F32 = jnp.float32
BF16 = jnp.bfloat16


def dot(a, b, dims=((1,), (0,))):
    return lax.dot_general(a, b, (dims, ((), ())), preferred_element_type=F32)


def layer_kernel(
    nz, row, ny,
    q_any, k_any, v_any, lens_any, gain_any, w_any, out_v,
    lens, gain, q_ref, k_ref, v_ref, s_loc, s_in, r_in, crow, c_out, c_in, lo_ref, within, norm_all, wcol, acc,
    load_sem, p1s, p1r, p2s, p2r, p3s, p3r, wys, wyr, wxs, wxr, wzs, wzr, wcs, wcr, ys, yr,
):
    tok, width = q_ref.shape
    heads = width // DH
    cols = out_v.shape[1]
    nx = row // 2
    yh, zh = ny // 2, nz // 2
    sl = width // row
    wr = width // nz
    xc = cols // nx
    seq, y = lax.axis_index("seq"), lax.axis_index("head")
    z, r = seq // row, seq % row
    x, c = r // 2, r % 2
    sends = []

    def remote(src, dst, ssem, rsem, target):
        return pltpu.make_async_remote_copy(
            src_ref=src, dst_ref=dst, send_sem=ssem, recv_sem=rsem,
            device_id=target, device_id_type=MESH)

    def send(*args):
        copy = remote(*args)
        copy.start()
        sends.append(copy)

    def row_dev(i):
        return (z * row + i, y)

    def z_dev(i):
        return (i * row + r, y)

    def y_dev(i):
        return (seq, i)

    barrier = pltpu.get_barrier_semaphore()
    def far_first(n):
        return sorted(range(1, n), key=lambda k: -min(k, n - k))

    peers = [z_dev((z + k) % nz) for k in far_first(nz)]
    peers += [y_dev((y + k) % ny) for k in far_first(ny)]
    peers += [row_dev((r + k) % row) for k in far_first(row)]
    r_in[...] = jnp.zeros_like(r_in)
    for peer in peers:
        pl.semaphore_signal(barrier, inc=1, device_id=peer, device_id_type=MESH)

    small = [
        pltpu.make_async_copy(lens_any, lens, load_sem.at[4]),
        pltpu.make_async_copy(gain_any, gain, load_sem.at[5]),
    ]
    loads = [
        pltpu.make_async_copy(k_any, k_ref, load_sem.at[0]),
        pltpu.make_async_copy(v_any, v_ref, load_sem.at[1]),
        pltpu.make_async_copy(q_any, q_ref, load_sem.at[2]),
        pltpu.make_async_copy(
            w_any.at[:, pl.ds(pl.multiple_of(y * cols, 128), cols)], wcol.at[0], load_sem.at[3]),
    ]
    for load in small[:1] + loads + small[1:]:
        load.start()

    small[0].wait()
    bounds, total = [], jnp.int32(0)
    for d in range(lens.shape[0]):
        total = total + lens[d]
        bounds.append(total)

    def start_of(position):
        found = jnp.int32(0)
        for bound in bounds:
            found = jnp.where(bound <= position, bound, found)
        return found

    def flag(condition):
        return jnp.where(condition, jnp.float32(1), jnp.float32(0))

    offset = seq * tok
    lo_last = start_of(offset + (tok - 1)) - offset
    first = z * row
    row_start = [start_of((first + i) * tok) for i in range(row)]
    next_start = start_of((first + row) * tok)
    w_row_sum = [flag((first + j + 1) * tok > next_start) for j in range(row)]
    w_past = [flag(row_start[i] < first * tok) for i in range(row)]
    w_rows = [flag(((i + 1) * row * tok > row_start[0]) & (i < z)) for i in range(nz)]

    rows = lax.broadcasted_iota(jnp.int32, (tok, DH), 0)
    keep = flag(rows >= lo_last)
    loads[0].wait()
    loads[1].wait()
    for h in range(heads):
        hs = slice(h * DH, (h + 1) * DH)
        key = (k_ref[:, hs].astype(F32) * keep).astype(BF16)
        s_loc[hs, :] = dot(key, v_ref[:, hs], ((0,), (0,))).astype(BF16)

    pl.semaphore_wait(barrier, len(peers))

    def part(i):
        return pl.ds(pl.multiple_of(i * sl, 16), sl)

    for k in far_first(row):
        i = (r + k) % row
        send(s_loc.at[part(i)], s_in.at[r], p1s.at[k], p1r.at[k], row_dev(i))

    first_rel = 1 + (yh - 1) * c
    z_rows = pl.ds(pl.multiple_of(z * wr, 16), wr)
    x_cols = pl.ds(pl.multiple_of(x * xc, 128), xc)
    for i in range(yh):
        rel = first_rel + i
        plane = (y + ny - rel) % ny
        send(
            w_any.at[z_rows, pl.ds(pl.multiple_of(plane * cols + x * xc, 128), xc)],
            wcol.at[rel, z_rows, x_cols], wys.at[i], wyr.at[i], y_dev(plane))

    s_in[r] = s_loc[part(r), :]
    lo = jnp.zeros((tok, DH), jnp.int32) - offset
    for bound in bounds:
        lo = jnp.where(rows >= bound - offset, bound - offset, lo)
    lo_ref[...] = lo
    loads[2].wait()

    tb = tok // 2

    def attend(h):
        hs = slice(h * DH, (h + 1) * DH)
        for b in range(2):
            upto = (b + 1) * tb
            ts = slice(b * tb, upto)
            scores = dot(q_ref[ts, hs], k_ref[:upto, hs], ((1,), (1,)))
            t_ids = lax.broadcasted_iota(jnp.int32, (tb, upto), 0) + b * tb
            s_ids = lax.broadcasted_iota(jnp.int32, (tb, upto), 1)
            low = jnp.broadcast_to(lo_ref[ts, 0:1], (tb, upto))
            allowed = (s_ids <= t_ids) & (s_ids >= low)
            scores = jnp.where(allowed, scores, 0.0).astype(BF16)
            within[h, ts, :] = dot(scores, v_ref[:upto, hs])

    attend(0)

    for k in range(1, row):
        j = (r + row - k) % row
        remote(s_loc.at[part(j)], s_in.at[j], p1s.at[k], p1r.at[k], row_dev(j)).wait_recv()

    state = [s_in[j].astype(F32) for j in range(row)]
    row_sum = functools.reduce(jnp.add, [w_row_sum[j] * state[j] for j in range(row)])
    r_in[z] = row_sum.astype(BF16)

    def p2_copy(k, i):
        return remote(r_in.at[i], r_in.at[i], p2s.at[k], p2r.at[k], z_dev((z + k) % nz))

    for k in far_first(nz):
        @pl.when(z + k < nz)
        def _():
            p2_copy(k, z).start()

    for i in range(row):
        total = jnp.zeros((sl, DH), F32)
        for j in range(i):
            total = total + flag((first + j + 1) * tok > row_start[i]) * state[j]
        crow[i] = total
    attend(1)

    for k in range(1, nz):
        @pl.when(z >= k)
        def _():
            p2_copy(k, (z + nz - k) % nz).wait_recv()

    past = functools.reduce(jnp.add, [w_rows[i] * r_in[i].astype(F32) for i in range(nz)])
    for i in range(row):
        c_out[i] = (crow[i] + w_past[i] * past).astype(BF16)
    for k in far_first(row):
        i = (r + k) % row
        send(c_out.at[i], c_in.at[part(r)], p3s.at[k], p3r.at[k], row_dev(i))
    c_in[part(r), :] = c_out[r]

    rels = pl.ds(first_rel, yh)
    for i in range(yh):
        rel = first_rel + i
        remote(
            w_any.at[z_rows, pl.ds(0, xc)], wcol.at[rel, z_rows, x_cols],
            wys.at[i], wyr.at[i], y_dev((y + rel) % ny)).wait_recv()
    for k in far_first(nx):
        block = wcol.at[rels, z_rows, x_cols]
        send(block, block, wxs.at[k], wxr.at[k], row_dev((x + k) % nx * 2 + c))

    attend(2)

    def z_block(i, first, count):
        return wcol.at[pl.ds(first, count), pl.ds(pl.multiple_of(i * wr, 16), wr), :]

    def z_copy(way, d, starting):
        step = 1 if way == 0 else nz - 1
        away = d if starting else d + 1
        owner = (z + away * (nz - step)) % nz
        if d < zh - 1:
            block = z_block(owner, first_rel, yh)
        elif way == 0:
            block = z_block(owner, first_rel, yh // 2)
        else:
            block = z_block(owner, first_rel + yh // 2, yh - yh // 2)
        return block, block, wzs.at[way, d], wzr.at[way, d], z_dev((z + step) % nz)

    own_rels, twin_rels = 1 + yh * c, 1 + yh * (1 - c)
    twin = row_dev(x * 2 + (1 - c))

    def to_twin(i, n):
        block = z_block(i, own_rels, yh - 1)
        send(block, block, wcs.at[n], wcr.at[n], twin)

    def z_step(d):
        if d > 0:
            for way in range(2):
                remote(*z_copy(way, d - 1, False)).wait_recv()
        if d < zh:
            for way in range(2):
                send(*z_copy(way, d, True))
        if d == 0 or d == zh:
            to_twin((z + d) % nz, d)
        else:
            to_twin((z + d) % nz, d)
            to_twin((z + nz - d) % nz, nz - d)

    def twin_wait():
        for n in range(nz):
            block = z_block((z + n) % nz, twin_rels, yh - 1)
            remote(block, block, wcs.at[n], wcr.at[n], twin).wait_recv()

    for k in range(1, row):
        j = (r + row - k) % row
        remote(c_out.at[j], c_in.at[part(j)], p3s.at[k], p3r.at[k], row_dev(j)).wait_recv()

    def y_copy(way, d, h, starting):
        slot = (ny - d) % ny if way == 0 else d
        later = ny - d - 1 if way == 0 else d + 1
        ts = pl.ds(0, tok)
        if d == yh - 1:
            ts = pl.ds(way * tb, tb)
        src, dst = norm_all.at[slot, h, ts], norm_all.at[later, h, ts]
        to = (y + 1) % ny if way == 0 else (y + ny - 1) % ny
        return src, dst, ys.at[way, d, h], yr.at[way, d, h], y_dev(to)

    def y_send(d, h):
        for way in range(2):
            send(*y_copy(way, d, h, True))

    def y_wait(d, h, ways=(0, 1)):
        for way in ways:
            remote(*y_copy(way, d - 1, h, False)).wait_recv()

    small[1].wait()
    for h in range(heads):
        hs = slice(h * DH, (h + 1) * DH)
        carried = c_in[hs, :]
        scale = jnp.broadcast_to(gain[hs][None, :], (tb, DH))
        for b in range(2):
            ts = slice(b * tb, (b + 1) * tb)
            term = dot(q_ref[ts, hs], carried)
            mixture = within[h, ts, :] + jnp.where(lo_ref[ts, :] < 0, term, 0.0)
            square_mean = jnp.mean(mixture * mixture, axis=-1, keepdims=True)
            norm_all[0, h, ts, :] = (mixture * lax.rsqrt(square_mean + 1e-06) * scale).astype(BF16)
        y_send(0, h)

    for k in range(1, nx):
        i = (x + nx - k) % nx
        block = wcol.at[rels, z_rows, pl.ds(pl.multiple_of(i * xc, 128), xc)]
        remote(block, block, wxs.at[k], wxr.at[k], row_dev(i * 2 + c)).wait_recv()

    z_step(0)

    def project(rel, start=False):
        for b in range(2):
            ts = slice(b * tb, (b + 1) * tb)
            left = jnp.concatenate([norm_all[rel, h, ts, :] for h in range(heads)], axis=1)
            term = dot(left, wcol[rel])
            acc[ts, :] = term if start else acc[ts, :] + term

    def y_step(d, h):
        y_wait(d, h)
        y_send(d, h)

    loads[3].wait()
    project(0, True)
    z_left = list(range(1, zh + 1))
    n = 0
    for d in range(1, yh):
        if d == yh - 1:
            while z_left:
                z_step(z_left.pop(0))
            twin_wait()
            for e in range(1, d):
                project(e)
                project(ny - e)
        for h in range(heads):
            y_step(d, h)
            n += 1
            if n in (1, 3, 5, 6) and z_left:
                z_step(z_left.pop(0))
    project(yh - 1)
    project(yh + 1)
    for h in range(heads):
        hs = slice(h * DH, (h + 1) * DH)
        for way in range(2):
            ts = slice(way * tb, (way + 1) * tb)
            y_wait(yh, h, (way,))
            total = acc[ts, :] + dot(norm_all[yh, h, ts, :], wcol[yh, hs, :])
            if h < heads - 1:
                acc[ts, :] = total
            else:
                out_v[ts, :] = total.astype(BF16)
    for copy in sends:
        copy.wait_send()
    for k in range(1, nz):
        @pl.when(z + k < nz)
        def _():
            p2_copy(k, z).wait_send()


def body(nz, row, ny, queries, key_vectors, value_vectors, doc_lengths, norm_gain, out_weight):
    tok, width = queries.shape
    heads = width // DH
    cols = out_weight.shape[1] // ny
    yh, zh = ny // 2, nz // 2
    sl = width // row
    dma = pltpu.SemaphoreType.DMA
    any_spec = pl.BlockSpec(memory_space=pl.ANY)
    return pl.pallas_call(
        functools.partial(layer_kernel, nz, row, ny),
        name="layer",
        out_shape=pltpu.VMEM((tok, cols), BF16),
        in_specs=[any_spec] * 6,
        out_specs=pl.BlockSpec(memory_space=pltpu.VMEM),
        scratch_shapes=[
            pltpu.SMEM(doc_lengths.shape, jnp.int32),
            pltpu.VMEM((width,), F32),
            pltpu.VMEM((tok, width), BF16),
            pltpu.VMEM((tok, width), BF16),
            pltpu.VMEM((tok, width), BF16),
            pltpu.VMEM((width, DH), BF16),
            pltpu.VMEM((row, sl, DH), BF16),
            pltpu.VMEM((nz, sl, DH), BF16),
            pltpu.VMEM((row, sl, DH), F32),
            pltpu.VMEM((row, sl, DH), BF16),
            pltpu.VMEM((width, DH), BF16),
            pltpu.VMEM((tok, DH), jnp.int32),
            pltpu.VMEM((heads, tok, DH), F32),
            pltpu.VMEM((ny, heads, tok, DH), BF16),
            pltpu.VMEM((ny, width, cols), BF16),
            pltpu.VMEM((tok, cols), F32),
            dma((6,)),
            dma((row,)), dma((row,)),
            dma((nz,)), dma((nz,)),
            dma((row,)), dma((row,)),
            dma((yh,)), dma((yh,)),
            dma((row // 2,)), dma((row // 2,)),
            dma((2, zh)), dma((2, zh)),
            dma((nz,)), dma((nz,)),
            dma((2, yh, heads)), dma((2, yh, heads)),
        ],
        compiler_params=pltpu.CompilerParams(collective_id=0, has_side_effects=True),
    )(queries, key_vectors, value_vectors, doc_lengths, norm_gain, out_weight)


def solution(mesh, row=ROW):
    nz, ny = mesh.shape["seq"] // row, mesh.shape["head"]
    return jax.shard_map(
        functools.partial(body, nz, row, ny),
        mesh=mesh,
        in_specs=(
            P("seq", "head"),
            P("seq", "head"),
            P("seq", "head"),
            P(),
            P("head"),
            P("head", None),
        ),
        out_specs=P("seq", "head"),
        check_vma=False,
    )
```

```python
import functools

import jax
import jax.numpy as jnp
from jax import lax
from jax.experimental import pallas as pl
from jax.experimental.pallas import tpu as pltpu
from jax.sharding import PartitionSpec as P

DH = 128
ROW = 8
MESH = pl.DeviceIdType.MESH
F32 = jnp.float32
BF16 = jnp.bfloat16


def dot(a, b, dims=((1,), (0,))):
    return lax.dot_general(a, b, (dims, ((), ())), preferred_element_type=F32)


def layer_kernel(
    nz, row, ny,
    q_any, k_any, v_any, lens_any, gain_any, w_any, out_v,
    lens, gain, q_ref, k_ref, v_ref, s_loc, s_in, r_in, crow, c_out, c_in, lo_ref, within, norm_all, wcol, acc,
    load_sem, p1s, p1r, p2s, p2r, p3s, p3r, wys, wyr, wzs, wzr, wcs, wcr, ys, yr,
):
    tok, width = q_ref.shape
    heads = width // DH
    cols = out_v.shape[1]
    yh, zh = ny // 2, nz // 2
    sl = DH // row
    wr = width // nz
    seq, y = lax.axis_index("seq"), lax.axis_index("head")
    z, r = seq // row, seq % row
    x, c = r // 2, r % 2
    sends = []

    def remote(src, dst, ssem, rsem, target):
        return pltpu.make_async_remote_copy(
            src_ref=src, dst_ref=dst, send_sem=ssem, recv_sem=rsem,
            device_id=target, device_id_type=MESH)

    def send(*args):
        copy = remote(*args)
        copy.start()
        sends.append(copy)

    def wait_bytes(ref, sem):
        pltpu.make_async_copy(ref, ref, sem).wait()

    def row_dev(i):
        return (z * row + i, y)

    def z_dev(i):
        return (i * row + r, y)

    def y_dev(i):
        return (seq, i)

    barrier = pltpu.get_barrier_semaphore()
    def far_first(n):
        return sorted(range(1, n), key=lambda k: -min(k, n - k))

    peers = [z_dev((z + k) % nz) for k in far_first(nz)]
    peers += [y_dev((y + k) % ny) for k in far_first(ny)]
    peers += [row_dev((r + k) % row) for k in far_first(row)]
    r_in[...] = jnp.zeros_like(r_in)
    for peer in peers:
        pl.semaphore_signal(barrier, inc=1, device_id=peer, device_id_type=MESH)

    small = [
        pltpu.make_async_copy(lens_any, lens, load_sem.at[4]),
        pltpu.make_async_copy(gain_any, gain, load_sem.at[5]),
    ]
    loads = [
        pltpu.make_async_copy(k_any, k_ref, load_sem.at[0]),
        pltpu.make_async_copy(v_any, v_ref, load_sem.at[1]),
        pltpu.make_async_copy(q_any, q_ref, load_sem.at[2]),
        pltpu.make_async_copy(
            w_any.at[:, pl.ds(pl.multiple_of(y * cols, 128), cols)], wcol.at[0], load_sem.at[3]),
    ]
    for load in small[:1] + loads + small[1:]:
        load.start()

    small[0].wait()
    bounds, total = [], jnp.int32(0)
    for d in range(lens.shape[0]):
        total = total + lens[d]
        bounds.append(total)

    def start_of(position):
        found = jnp.int32(0)
        for bound in bounds:
            found = jnp.where(bound <= position, bound, found)
        return found

    def flag(condition):
        return jnp.where(condition, jnp.float32(1), jnp.float32(0))

    offset = seq * tok
    lo_last = start_of(offset + (tok - 1)) - offset
    first = z * row
    row_start = [start_of((first + i) * tok) for i in range(row)]
    next_start = start_of((first + row) * tok)
    w_row_sum = [flag((first + j + 1) * tok > next_start) for j in range(row)]
    w_past = [flag(row_start[i] < first * tok) for i in range(row)]
    w_rows = [flag(((i + 1) * row * tok > row_start[0]) & (i < z)) for i in range(nz)]

    rows = lax.broadcasted_iota(jnp.int32, (tok, DH), 0)
    keep = flag(rows >= lo_last)
    loads[0].wait()
    loads[1].wait()
    for h in range(heads):
        hs = slice(h * DH, (h + 1) * DH)
        key = (k_ref[:, hs].astype(F32) * keep).astype(BF16)
        s_loc[h] = dot(key, v_ref[:, hs], ((0,), (0,))).astype(BF16)

    pl.semaphore_wait(barrier, len(peers))

    def part(i):
        return pl.ds(pl.multiple_of(i * sl, 16), sl)

    for h in range(heads):
        for k in far_first(row):
            i = (r + k) % row
            remote(s_loc.at[h, part(i)], s_in.at[h, r], p1s.at[h], p1r.at[h], row_dev(i)).start()

    first_rel = 1 + (yh - 1) * c
    z_rows = pl.ds(pl.multiple_of(z * wr, 16), wr)
    for i in range(yh):
        rel = first_rel + i
        plane = (y + ny - rel) % ny
        remote(
            w_any.at[z_rows, pl.ds(pl.multiple_of(plane * cols, 128), cols)],
            wcol.at[rel, z_rows, :], wys, wyr, y_dev(plane)).start()

    for h in range(heads):
        s_in[h, r] = s_loc[h, part(r), :]
    lo = jnp.zeros((tok, DH), jnp.int32) - offset
    for bound in bounds:
        lo = jnp.where(rows >= bound - offset, bound - offset, lo)
    lo_ref[...] = lo
    loads[2].wait()

    tb = tok // 2

    def attend(h):
        hs = slice(h * DH, (h + 1) * DH)
        for b in range(2):
            upto = (b + 1) * tb
            ts = slice(b * tb, upto)
            scores = dot(q_ref[ts, hs], k_ref[:upto, hs], ((1,), (1,)))
            t_ids = lax.broadcasted_iota(jnp.int32, (tb, upto), 0) + b * tb
            s_ids = lax.broadcasted_iota(jnp.int32, (tb, upto), 1)
            low = jnp.broadcast_to(lo_ref[ts, 0:1], (tb, upto))
            allowed = (s_ids <= t_ids) & (s_ids >= low)
            scores = jnp.where(allowed, scores, 0.0).astype(BF16)
            within[h, ts, :] = dot(scores, v_ref[:upto, hs])

    attend(0)

    def p2_copy(h, k, i):
        return remote(
            r_in.at[h, i], r_in.at[h, i], p2s.at[h, k], p2r.at[h, k], z_dev((z + k) % nz))

    others = pl.ds(0, row - 1)
    for h in range(heads):
        wait_bytes(s_in.at[h, others], p1r.at[h])
        row_sum = functools.reduce(
            jnp.add, [w_row_sum[j] * s_in[h, j].astype(F32) for j in range(row)])
        r_in[h, z] = row_sum.astype(BF16)
        for k in far_first(nz):
            @pl.when(z + k < nz)
            def _():
                p2_copy(h, k, z).start()

    w_own = {
        (i, j): flag((first + j + 1) * tok > row_start[i]) for i in range(row) for j in range(i)}
    for h in range(heads):
        state = [s_in[h, j].astype(F32) for j in range(row)]
        for i in range(row):
            total = jnp.zeros((sl, DH), F32)
            for j in range(i):
                total = total + w_own[i, j] * state[j]
            crow[h, i] = total
    attend(1)

    for h in range(heads):
        for k in range(1, nz):
            @pl.when(z >= k)
            def _():
                p2_copy(h, k, (z + nz - k) % nz).wait_recv()
        past = functools.reduce(
            jnp.add, [w_rows[i] * r_in[h, i].astype(F32) for i in range(nz)])
        for i in range(row):
            c_out[h, i] = (crow[h, i] + w_past[i] * past).astype(BF16)
        for k in far_first(row):
            i = (r + k) % row
            remote(c_out.at[h, i], c_in.at[h, part(r)], p3s.at[h], p3r.at[h], row_dev(i)).start()
        c_in[h, part(r), :] = c_out[h, r]

    attend(2)

    def z_block(i, first, count):
        return wcol.at[pl.ds(first, count), pl.ds(pl.multiple_of(i * wr, 16), wr), :]

    def z_copy(way, d, half, starting):
        step = 1 if way == 0 else nz - 1
        away = d if starting else d + 1
        owner = (z + away * (nz - step)) % nz
        count = yh // 2 if half == 0 else yh - yh // 2
        block = z_block(owner, first_rel + half * (yh // 2), count)
        return block, block, wzs.at[way, half, d], wzr.at[way, half, d], z_dev((z + step) % nz)

    own_rels, twin_rels = 1 + yh * c, 1 + yh * (1 - c)
    twin = row_dev(x * 2 + (1 - c))

    def to_twin(i):
        block = z_block(i, own_rels, yh - 1)
        remote(block, block, wcs, wcr, twin).start()

    def z_step(d, half):
        for way in range(2):
            if d > 0 and (d < zh or way == half):
                remote(*z_copy(way, d - 1, half, False)).wait_recv()
        for way in range(2):
            if d < zh - 1 or (d == zh - 1 and way == half):
                send(*z_copy(way, d, half, True))
        if half == 1:
            to_twin((z + d) % nz)
            if 0 < d < zh:
                to_twin((z + nz - d) % nz)

    def y_copy(way, d, h, starting):
        slot = (ny - d) % ny if way == 0 else d
        later = ny - d - 1 if way == 0 else d + 1
        ts = pl.ds(0, tok)
        if d == yh - 1:
            ts = pl.ds(way * tb, tb)
        src, dst = norm_all.at[slot, h, ts], norm_all.at[later, h, ts]
        to = (y + 1) % ny if way == 0 else (y + ny - 1) % ny
        return src, dst, ys.at[way, d, h], yr.at[way, d, h], y_dev(to)

    def y_send(d, h):
        for way in range(2):
            send(*y_copy(way, d, h, True))

    def y_wait(d, h, ways=(0, 1)):
        for way in ways:
            remote(*y_copy(way, d - 1, h, False)).wait_recv()

    small[1].wait()
    for h in range(heads):
        hs = slice(h * DH, (h + 1) * DH)
        wait_bytes(c_in.at[h, pl.ds(0, sl * (row - 1))], p3r.at[h])
        carried = c_in[h]
        scale = jnp.broadcast_to(gain[hs][None, :], (tb, DH))
        for b in range(2):
            ts = slice(b * tb, (b + 1) * tb)
            term = dot(q_ref[ts, hs], carried)
            mixture = within[h, ts, :] + jnp.where(lo_ref[ts, :] < 0, term, 0.0)
            square_mean = jnp.mean(mixture * mixture, axis=-1, keepdims=True)
            norm_all[0, h, ts, :] = (mixture * lax.rsqrt(square_mean + 1e-06) * scale).astype(BF16)
        y_send(0, h)

    def project(rel, start=False):
        for b in range(2):
            ts = slice(b * tb, (b + 1) * tb)
            left = jnp.concatenate([norm_all[rel, h, ts, :] for h in range(heads)], axis=1)
            term = dot(left, wcol[rel])
            acc[ts, :] = term if start else acc[ts, :] + term

    def y_step(d, h):
        y_wait(d, h)
        y_send(d, h)

    loads[3].wait()
    project(0, True)
    y_events = [(d, h) for d in range(1, yh) for h in range(heads)]
    z_events = [(d, half) for d in range(1, zh + 1) for half in range(2)]
    z_after = [min(2 + m * 3 // 4, len(y_events) - 2) for m in range(len(z_events))]
    for n, (d, h) in enumerate(y_events):
        y_step(d, h)
        if n == 0:
            wait_bytes(z_block(z, first_rel, yh), wyr)
            z_step(0, 0)
            z_step(0, 1)
        for after, event in zip(z_after, z_events):
            if after == n:
                z_step(*event)
        if n == 2:
            for h2 in range(heads):
                wait_bytes(s_in.at[h2, others], p1s.at[h2])
                wait_bytes(s_in.at[h2, others], p3s.at[h2])
                for k in range(1, nz):
                    @pl.when(z + k < nz)
                    def _():
                        p2_copy(h2, k, z).wait_send()
            wait_bytes(z_block(z, first_rel, yh), wys)
        if n == len(y_events) // 2:
            early = len(sends)
        if n == len(y_events) - 1:
            wait_bytes(wcol.at[pl.ds(twin_rels, yh - 1)], wcr)
            wait_bytes(wcol.at[pl.ds(own_rels, yh - 1)], wcs)
            for copy in sends[:early]:
                copy.wait_send()
            for e in range(1, yh - 1):
                project(e)
                project(ny - e)
    project(yh - 1)
    project(yh + 1)
    for h in range(heads):
        hs = slice(h * DH, (h + 1) * DH)
        for way in range(2):
            ts = slice(way * tb, (way + 1) * tb)
            y_wait(yh, h, (way,))
            total = acc[ts, :] + dot(norm_all[yh, h, ts, :], wcol[yh, hs, :])
            if h < heads - 1:
                acc[ts, :] = total
            else:
                out_v[ts, :] = total.astype(BF16)
    for copy in sends[early:]:
        copy.wait_send()


def body(nz, row, ny, queries, key_vectors, value_vectors, doc_lengths, norm_gain, out_weight):
    tok, width = queries.shape
    heads = width // DH
    cols = out_weight.shape[1] // ny
    yh, zh = ny // 2, nz // 2
    sl = DH // row
    dma = pltpu.SemaphoreType.DMA
    any_spec = pl.BlockSpec(memory_space=pl.ANY)
    return pl.pallas_call(
        functools.partial(layer_kernel, nz, row, ny),
        name="layer",
        out_shape=pltpu.VMEM((tok, cols), BF16),
        in_specs=[any_spec] * 6,
        out_specs=pl.BlockSpec(memory_space=pltpu.VMEM),
        scratch_shapes=[
            pltpu.SMEM(doc_lengths.shape, jnp.int32),
            pltpu.VMEM((width,), F32),
            pltpu.VMEM((tok, width), BF16),
            pltpu.VMEM((tok, width), BF16),
            pltpu.VMEM((tok, width), BF16),
            pltpu.VMEM((heads, DH, DH), BF16),
            pltpu.VMEM((heads, row, sl, DH), BF16),
            pltpu.VMEM((heads, nz, sl, DH), BF16),
            pltpu.VMEM((heads, row, sl, DH), F32),
            pltpu.VMEM((heads, row, sl, DH), BF16),
            pltpu.VMEM((heads, DH, DH), BF16),
            pltpu.VMEM((tok, DH), jnp.int32),
            pltpu.VMEM((heads, tok, DH), F32),
            pltpu.VMEM((ny, heads, tok, DH), BF16),
            pltpu.VMEM((ny, width, cols), BF16),
            pltpu.VMEM((tok, cols), F32),
            dma((6,)),
            dma((heads,)), dma((heads,)),
            dma((heads, nz)), dma((heads, nz)),
            dma((heads,)), dma((heads,)),
            dma(()), dma(()),
            dma((2, 2, zh)), dma((2, 2, zh)),
            dma(()), dma(()),
            dma((2, yh, heads)), dma((2, yh, heads)),
        ],
        compiler_params=pltpu.CompilerParams(collective_id=0, has_side_effects=True),
    )(queries, key_vectors, value_vectors, doc_lengths, norm_gain, out_weight)


def solution(mesh, row=ROW):
    nz, ny = mesh.shape["seq"] // row, mesh.shape["head"]
    return jax.shard_map(
        functools.partial(body, nz, row, ny),
        mesh=mesh,
        in_specs=(
            P("seq", "head"),
            P("seq", "head"),
            P("seq", "head"),
            P(),
            P("head"),
            P("head", None),
        ),
        out_specs=P("seq", "head"),
        check_vma=False,
    )
```

```python
import functools

import jax
import jax.numpy as jnp
from jax import lax
from jax.experimental import pallas as pl
from jax.experimental.pallas import tpu as pltpu
from jax.sharding import PartitionSpec as P

DH = 128
ROW = 8
MESH = pl.DeviceIdType.MESH
F32 = jnp.float32
BF16 = jnp.bfloat16


def dot(a, b, dims=((1,), (0,))):
    return lax.dot_general(a, b, (dims, ((), ())), preferred_element_type=F32)


def layer_kernel(
    nz, row, ny,
    q_any, k_any, v_any, lens_any, gain_any, w_any, out_v,
    lens, gain, q_ref, k_ref, v_ref, s_loc, s_in, r_in, crow, c_out, c_in, lo_ref, within, norm_all, wcol, acc,
    load_sem, p1s, p1r, p2s, p2r, p3s, p3r, wys, wyr, wzs, wzr, wcs, wcr, ys, yr, z_level, y_level,
):
    tok, width = q_ref.shape
    heads = width // DH
    cols = out_v.shape[1]
    yh, zh = ny // 2, nz // 2
    sl = DH // row
    wr = width // nz
    seq, y = lax.axis_index("seq"), lax.axis_index("head")
    z, r = seq // row, seq % row
    x, c = r // 2, r % 2
    sends = []

    def remote(src, dst, ssem, rsem, target):
        return pltpu.make_async_remote_copy(
            src_ref=src, dst_ref=dst, send_sem=ssem, recv_sem=rsem,
            device_id=target, device_id_type=MESH)

    def send(*args):
        copy = remote(*args)
        copy.start()
        sends.append(copy)

    def wait_bytes(ref, sem):
        pltpu.make_async_copy(ref, ref, sem).wait()

    def row_dev(i):
        return (z * row + i, y)

    def z_dev(i):
        return (i * row + r, y)

    def y_dev(i):
        return (seq, i)

    barrier = pltpu.get_barrier_semaphore()
    def far_first(n):
        return sorted(range(1, n), key=lambda k: -min(k, n - k))

    z_near = [z_dev((z + 1) % nz), z_dev((z + nz - 1) % nz)]
    y_near = [y_dev((y + 1) % ny), y_dev((y + ny - 1) % ny)]
    peers = z_near + y_near + [row_dev((r + k) % row) for k in far_first(row)]
    r_in[...] = jnp.zeros_like(r_in)
    for peer in peers:
        pl.semaphore_signal(barrier, inc=1, device_id=peer, device_id_type=MESH)

    small = [
        pltpu.make_async_copy(lens_any, lens, load_sem.at[4]),
        pltpu.make_async_copy(gain_any, gain, load_sem.at[5]),
    ]
    loads = [
        pltpu.make_async_copy(k_any, k_ref, load_sem.at[0]),
        pltpu.make_async_copy(v_any, v_ref, load_sem.at[1]),
        pltpu.make_async_copy(q_any, q_ref, load_sem.at[2]),
        pltpu.make_async_copy(
            w_any.at[:, pl.ds(pl.multiple_of(y * cols, 128), cols)], wcol.at[0], load_sem.at[3]),
    ]
    for load in small[:1] + loads + small[1:]:
        load.start()

    small[0].wait()
    bounds, total = [], jnp.int32(0)
    for d in range(lens.shape[0]):
        total = total + lens[d]
        bounds.append(total)

    def start_of(position):
        found = jnp.int32(0)
        for bound in bounds:
            found = jnp.where(bound <= position, bound, found)
        return found

    def flag(condition):
        return jnp.where(condition, jnp.float32(1), jnp.float32(0))

    offset = seq * tok
    lo_last = start_of(offset + (tok - 1)) - offset
    first = z * row
    row_start = [start_of((first + i) * tok) for i in range(row)]
    next_start = start_of((first + row) * tok)
    w_row_sum = [flag((first + j + 1) * tok > next_start) for j in range(row)]
    w_past = [flag(row_start[i] < first * tok) for i in range(row)]
    w_rows = [flag(((i + 1) * row * tok > row_start[0]) & (i < z)) for i in range(nz)]

    rows = lax.broadcasted_iota(jnp.int32, (tok, DH), 0)
    keep = flag(rows >= lo_last)
    loads[0].wait()
    loads[1].wait()
    for h in range(heads):
        hs = slice(h * DH, (h + 1) * DH)
        key = (k_ref[:, hs].astype(F32) * keep).astype(BF16)
        s_loc[h] = dot(key, v_ref[:, hs], ((0,), (0,))).astype(BF16)

    pl.semaphore_wait(barrier, len(peers))

    def tell(near, level):
        for peer in near:
            pl.semaphore_signal(level, inc=1, device_id=peer, device_id_type=MESH)

    def relay(near, levels, n, last):
        pl.semaphore_wait(levels.at[n], 2)
        if n < last - 1:
            tell(near, levels.at[n + 1])

    def part(i):
        return pl.ds(pl.multiple_of(i * sl, 16), sl)

    for h in range(heads):
        for k in far_first(row):
            i = (r + k) % row
            remote(s_loc.at[h, part(i)], s_in.at[h, r], p1s.at[h], p1r.at[h], row_dev(i)).start()

    first_rel = 1 + (yh - 1) * c
    z_rows = pl.ds(pl.multiple_of(z * wr, 16), wr)
    tell(z_near, z_level.at[0])
    tell(y_near, y_level.at[0])
    for h in range(heads):
        s_in[h, r] = s_loc[h, part(r), :]
    lo = jnp.zeros((tok, DH), jnp.int32) - offset
    for bound in bounds:
        lo = jnp.where(rows >= bound - offset, bound - offset, lo)
    lo_ref[...] = lo
    loads[2].wait()

    tb = tok // 2

    def attend(h):
        hs = slice(h * DH, (h + 1) * DH)
        for b in range(2):
            upto = (b + 1) * tb
            ts = slice(b * tb, upto)
            scores = dot(q_ref[ts, hs], k_ref[:upto, hs], ((1,), (1,)))
            t_ids = lax.broadcasted_iota(jnp.int32, (tb, upto), 0) + b * tb
            s_ids = lax.broadcasted_iota(jnp.int32, (tb, upto), 1)
            low = jnp.broadcast_to(lo_ref[ts, 0:1], (tb, upto))
            allowed = (s_ids <= t_ids) & (s_ids >= low)
            scores = jnp.where(allowed, scores, 0.0).astype(BF16)
            within[h, ts, :] = dot(scores, v_ref[:upto, hs])

    relay(z_near, z_level, 0, zh - 1)
    attend(0)
    for n in range(1, zh - 1):
        relay(z_near, z_level, n, zh - 1)

    def p2_copy(h, k, i):
        return remote(
            r_in.at[h, i], r_in.at[h, i], p2s.at[h, k], p2r.at[h, k], z_dev((z + k) % nz))

    others = pl.ds(0, row - 1)
    for h in range(heads):
        wait_bytes(s_in.at[h, others], p1r.at[h])
        row_sum = functools.reduce(
            jnp.add, [w_row_sum[j] * s_in[h, j].astype(F32) for j in range(row)])
        r_in[h, z] = row_sum.astype(BF16)
        for k in far_first(nz):
            @pl.when(z + k < nz)
            def _():
                p2_copy(h, k, z).start()

    for n in range(yh - 1):
        relay(y_near, y_level, n, yh - 1)
    for i in range(yh):
        rel = first_rel + i
        plane = (y + ny - rel) % ny
        remote(
            w_any.at[z_rows, pl.ds(pl.multiple_of(plane * cols, 128), cols)],
            wcol.at[rel, z_rows, :], wys, wyr, y_dev(plane)).start()
    w_own = {
        (i, j): flag((first + j + 1) * tok > row_start[i]) for i in range(row) for j in range(i)}
    for h in range(heads):
        state = [s_in[h, j].astype(F32) for j in range(row)]
        for i in range(row):
            total = jnp.zeros((sl, DH), F32)
            for j in range(i):
                total = total + w_own[i, j] * state[j]
            crow[h, i] = total
    attend(1)

    for h in range(heads):
        for k in range(1, nz):
            @pl.when(z >= k)
            def _():
                p2_copy(h, k, (z + nz - k) % nz).wait_recv()
        past = functools.reduce(
            jnp.add, [w_rows[i] * r_in[h, i].astype(F32) for i in range(nz)])
        for i in range(row):
            c_out[h, i] = (crow[h, i] + w_past[i] * past).astype(BF16)
        for k in far_first(row):
            i = (r + k) % row
            remote(c_out.at[h, i], c_in.at[h, part(r)], p3s.at[h], p3r.at[h], row_dev(i)).start()
        c_in[h, part(r), :] = c_out[h, r]

    attend(2)

    def z_block(i, first, count):
        return wcol.at[pl.ds(first, count), pl.ds(pl.multiple_of(i * wr, 16), wr), :]

    def z_copy(way, d, half, starting):
        step = 1 if way == 0 else nz - 1
        away = d if starting else d + 1
        owner = (z + away * (nz - step)) % nz
        count = yh // 2 if half == 0 else yh - yh // 2
        block = z_block(owner, first_rel + half * (yh // 2), count)
        return block, block, wzs.at[way, half, d], wzr.at[way, half, d], z_dev((z + step) % nz)

    own_rels, twin_rels = 1 + yh * c, 1 + yh * (1 - c)
    twin = row_dev(x * 2 + (1 - c))

    def to_twin(i):
        block = z_block(i, own_rels, yh - 1)
        remote(block, block, wcs, wcr, twin).start()

    def z_step(d, half):
        for way in range(2):
            if d > 0 and (d < zh or way == half):
                remote(*z_copy(way, d - 1, half, False)).wait_recv()
        for way in range(2):
            if d < zh - 1 or (d == zh - 1 and way == half):
                send(*z_copy(way, d, half, True))
        if half == 1:
            to_twin((z + d) % nz)
            if 0 < d < zh:
                to_twin((z + nz - d) % nz)

    def y_copy(way, d, h, starting):
        slot = (ny - d) % ny if way == 0 else d
        later = ny - d - 1 if way == 0 else d + 1
        ts = pl.ds(0, tok)
        if d == yh - 1:
            ts = pl.ds(way * tb, tb)
        src, dst = norm_all.at[slot, h, ts], norm_all.at[later, h, ts]
        to = (y + 1) % ny if way == 0 else (y + ny - 1) % ny
        return src, dst, ys.at[way, d, h], yr.at[way, d, h], y_dev(to)

    def y_send(d, h):
        for way in range(2):
            send(*y_copy(way, d, h, True))

    def y_wait(d, h, ways=(0, 1)):
        for way in ways:
            remote(*y_copy(way, d - 1, h, False)).wait_recv()

    small[1].wait()
    for h in range(heads):
        hs = slice(h * DH, (h + 1) * DH)
        wait_bytes(c_in.at[h, pl.ds(0, sl * (row - 1))], p3r.at[h])
        carried = c_in[h]
        scale = jnp.broadcast_to(gain[hs][None, :], (tb, DH))
        for b in range(2):
            ts = slice(b * tb, (b + 1) * tb)
            term = dot(q_ref[ts, hs], carried)
            mixture = within[h, ts, :] + jnp.where(lo_ref[ts, :] < 0, term, 0.0)
            square_mean = jnp.mean(mixture * mixture, axis=-1, keepdims=True)
            norm_all[0, h, ts, :] = (mixture * lax.rsqrt(square_mean + 1e-06) * scale).astype(BF16)
        y_send(0, h)

    def project(rel, start=False):
        for b in range(2):
            ts = slice(b * tb, (b + 1) * tb)
            left = jnp.concatenate([norm_all[rel, h, ts, :] for h in range(heads)], axis=1)
            term = dot(left, wcol[rel])
            acc[ts, :] = term if start else acc[ts, :] + term

    def y_step(d, h):
        y_wait(d, h)
        y_send(d, h)

    wait_bytes(z_block(z, first_rel, yh), wyr)
    z_step(0, 0)
    z_step(0, 1)
    loads[3].wait()
    project(0, True)
    y_events = [(d, h) for d in range(1, yh) for h in range(heads)]
    z_events = [(d, half) for d in range(1, zh + 1) for half in range(2)]
    z_after = [min(m, len(y_events) - 3) for m in range(len(z_events))]
    for n, (d, h) in enumerate(y_events):
        y_step(d, h)
        for after, event in zip(z_after, z_events):
            if after == n:
                z_step(*event)
        if n == 2:
            for h2 in range(heads):
                wait_bytes(s_in.at[h2, others], p1s.at[h2])
                wait_bytes(s_in.at[h2, others], p3s.at[h2])
                for k in range(1, nz):
                    @pl.when(z + k < nz)
                    def _():
                        p2_copy(h2, k, z).wait_send()
            wait_bytes(z_block(z, first_rel, yh), wys)
        if n == len(y_events) // 2:
            early = len(sends)
        if n == len(y_events) - 1:
            wait_bytes(wcol.at[pl.ds(twin_rels, yh - 1)], wcr)
            wait_bytes(wcol.at[pl.ds(own_rels, yh - 1)], wcs)
            for copy in sends[:early]:
                copy.wait_send()
            for e in range(1, yh - 1):
                project(e)
                project(ny - e)
    project(yh - 1)
    project(yh + 1)
    for h in range(heads):
        hs = slice(h * DH, (h + 1) * DH)
        for way in range(2):
            ts = slice(way * tb, (way + 1) * tb)
            y_wait(yh, h, (way,))
            total = acc[ts, :] + dot(norm_all[yh, h, ts, :], wcol[yh, hs, :])
            if h < heads - 1:
                acc[ts, :] = total
            else:
                out_v[ts, :] = total.astype(BF16)
    for copy in sends[early:]:
        copy.wait_send()


def body(nz, row, ny, queries, key_vectors, value_vectors, doc_lengths, norm_gain, out_weight):
    tok, width = queries.shape
    heads = width // DH
    cols = out_weight.shape[1] // ny
    yh, zh = ny // 2, nz // 2
    sl = DH // row
    dma = pltpu.SemaphoreType.DMA
    any_spec = pl.BlockSpec(memory_space=pl.ANY)
    return pl.pallas_call(
        functools.partial(layer_kernel, nz, row, ny),
        name="layer",
        out_shape=pltpu.VMEM((tok, cols), BF16),
        in_specs=[any_spec] * 6,
        out_specs=pl.BlockSpec(memory_space=pltpu.VMEM),
        scratch_shapes=[
            pltpu.SMEM(doc_lengths.shape, jnp.int32),
            pltpu.VMEM((width,), F32),
            pltpu.VMEM((tok, width), BF16),
            pltpu.VMEM((tok, width), BF16),
            pltpu.VMEM((tok, width), BF16),
            pltpu.VMEM((heads, DH, DH), BF16),
            pltpu.VMEM((heads, row, sl, DH), BF16),
            pltpu.VMEM((heads, nz, sl, DH), BF16),
            pltpu.VMEM((heads, row, sl, DH), F32),
            pltpu.VMEM((heads, row, sl, DH), BF16),
            pltpu.VMEM((heads, DH, DH), BF16),
            pltpu.VMEM((tok, DH), jnp.int32),
            pltpu.VMEM((heads, tok, DH), F32),
            pltpu.VMEM((ny, heads, tok, DH), BF16),
            pltpu.VMEM((ny, width, cols), BF16),
            pltpu.VMEM((tok, cols), F32),
            dma((6,)),
            dma((heads,)), dma((heads,)),
            dma((heads, nz)), dma((heads, nz)),
            dma((heads,)), dma((heads,)),
            dma(()), dma(()),
            dma((2, 2, zh)), dma((2, 2, zh)),
            dma(()), dma(()),
            dma((2, yh, heads)), dma((2, yh, heads)),
            pltpu.SemaphoreType.REGULAR((zh - 1,)),
            pltpu.SemaphoreType.REGULAR((yh - 1,)),
        ],
        compiler_params=pltpu.CompilerParams(collective_id=0, has_side_effects=True),
    )(queries, key_vectors, value_vectors, doc_lengths, norm_gain, out_weight)


def solution(mesh, row=ROW):
    nz, ny = mesh.shape["seq"] // row, mesh.shape["head"]
    return jax.shard_map(
        functools.partial(body, nz, row, ny),
        mesh=mesh,
        in_specs=(
            P("seq", "head"),
            P("seq", "head"),
            P("seq", "head"),
            P(),
            P("head"),
            P("head", None),
        ),
        out_specs=P("seq", "head"),
        check_vma=False,
    )
```

```python
import functools

import jax
import jax.numpy as jnp
from jax import lax
from jax.experimental import pallas as pl
from jax.experimental.pallas import tpu as pltpu
from jax.sharding import PartitionSpec as P

DH = 128
ROW = 8
MESH = pl.DeviceIdType.MESH
F32 = jnp.float32
BF16 = jnp.bfloat16


def dot(a, b, dims=((1,), (0,))):
    return lax.dot_general(a, b, (dims, ((), ())), preferred_element_type=F32)


def layer_kernel(
    nz, row, ny,
    q_any, k_any, v_any, lens_any, gain_any, w_any, out_v,
    lens, gain, q_ref, k_ref, v_ref, s_loc, s_in, r_in, crow, c_out, c_in, lo_ref, within, within_0, q_near, in_near, c_near, g_below, g_above, norm_all, wcol, acc,
    load_sem, p1s, p1r, p2s, p2r, p3s, p3r, wys, wyr, wzs, wzr, wcs, wcr, ys, yr, es, er,
):
    tok, width = q_ref.shape
    heads = width // DH
    cols = out_v.shape[1]
    yh, zh = ny // 2, nz // 2
    sl = DH // row
    wr = width // nz
    seq, y = lax.axis_index("seq"), lax.axis_index("head")
    z, r = seq // row, seq % row
    x, c = r // 2, r % 2
    sends = []

    def remote(src, dst, ssem, rsem, target):
        return pltpu.make_async_remote_copy(
            src_ref=src, dst_ref=dst, send_sem=ssem, recv_sem=rsem,
            device_id=target, device_id_type=MESH)

    def send(*args):
        copy = remote(*args)
        copy.start()
        sends.append(copy)

    def wait_bytes(ref, sem):
        pltpu.make_async_copy(ref, ref, sem).wait()

    def row_dev(i):
        return (z * row + i, y)

    def z_dev(i):
        return (i * row + r, y)

    def y_dev(i):
        return (seq, i)

    barrier = pltpu.get_barrier_semaphore()
    def far_first(n):
        return sorted(range(1, n), key=lambda k: -min(k, n - k))

    peers = [z_dev((z + k) % nz) for k in far_first(nz)]
    peers += [y_dev((y + k) % ny) for k in far_first(ny)]
    peers += [row_dev((r + k) % row) for k in far_first(row)]
    r_in[...] = jnp.zeros_like(r_in)
    for peer in peers:
        pl.semaphore_signal(barrier, inc=1, device_id=peer, device_id_type=MESH)

    small = [
        pltpu.make_async_copy(lens_any, lens, load_sem.at[4]),
        pltpu.make_async_copy(gain_any, gain, load_sem.at[5]),
    ]
    loads = [
        pltpu.make_async_copy(k_any, k_ref, load_sem.at[0]),
        pltpu.make_async_copy(v_any, v_ref, load_sem.at[1]),
        pltpu.make_async_copy(q_any, q_ref, load_sem.at[2]),
        pltpu.make_async_copy(
            w_any.at[:, pl.ds(pl.multiple_of(y * cols, 128), cols)], wcol.at[0], load_sem.at[3]),
    ]
    for load in small[:1] + loads + small[1:]:
        load.start()

    small[0].wait()
    bounds, total = [], jnp.int32(0)
    for d in range(lens.shape[0]):
        total = total + lens[d]
        bounds.append(total)

    def start_of(position):
        found = jnp.int32(0)
        for bound in bounds:
            found = jnp.where(bound <= position, bound, found)
        return found

    def flag(condition):
        return jnp.where(condition, jnp.float32(1), jnp.float32(0))

    offset = seq * tok
    lo_last = start_of(offset + (tok - 1)) - offset
    first = z * row
    row_start = [start_of((first + i) * tok) for i in range(row)]
    next_start = start_of((first + row) * tok)
    w_row_sum = [flag((first + j + 1) * tok > next_start) for j in range(row)]
    w_past = [flag(row_start[i] < first * tok) for i in range(row)]
    w_rows = [flag(((i + 1) * row * tok > row_start[0]) & (i < z)) for i in range(nz)]

    rows = lax.broadcasted_iota(jnp.int32, (tok, DH), 0)
    keep = flag(rows >= lo_last)
    loads[0].wait()
    loads[1].wait()
    for h in range(heads):
        hs = slice(h * DH, (h + 1) * DH)
        key = (k_ref[:, hs].astype(F32) * keep).astype(BF16)
        s_loc[h] = dot(key, v_ref[:, hs], ((0,), (0,))).astype(BF16)

    pl.semaphore_wait(barrier, len(peers))

    def part(i):
        return pl.ds(pl.multiple_of(i * sl, 16), sl)

    for h in range(heads):
        for k in far_first(row):
            i = (r + k) % row
            remote(s_loc.at[h, part(i)], s_in.at[h, r], p1s.at[h], p1r.at[h], row_dev(i)).start()

    y_near = (y_dev((y + 1) % ny), y_dev((y + ny - 1) % ny))
    g_near = (g_below, g_above)

    def near_copy(way, kind):
        src, dst = (
            (q_ref.at[:, pl.ds(0, DH)], q_near.at[way]),
            (gain, g_near[way]),
            (within_0, in_near.at[way]),
            (c_in.at[0], c_near.at[way]),
        )[kind]
        return remote(src, dst, es.at[way, kind], er.at[way, kind], y_near[way])

    def near_send(kind):
        for way in range(2):
            near_copy(way, kind).start()

    loads[2].wait()
    near_send(0)
    small[1].wait()
    near_send(1)

    first_rel = 1 + (yh - 1) * c
    z_rows = pl.ds(pl.multiple_of(z * wr, 16), wr)
    for i in range(yh):
        rel = yh + i * (2 * c - 1)
        plane = (y + ny - rel) % ny
        remote(
            w_any.at[z_rows, pl.ds(pl.multiple_of(plane * cols, 128), cols)],
            wcol.at[rel, z_rows, :], wys, wyr, y_dev(plane)).start()

    for h in range(heads):
        s_in[h, r] = s_loc[h, part(r), :]
    lo = jnp.zeros((tok, DH), jnp.int32) - offset
    for bound in bounds:
        lo = jnp.where(rows >= bound - offset, bound - offset, lo)
    lo_ref[...] = lo

    tb = tok // 2

    def attend(h):
        hs = slice(h * DH, (h + 1) * DH)
        for b in range(2):
            upto = (b + 1) * tb
            ts = slice(b * tb, upto)
            scores = dot(q_ref[ts, hs], k_ref[:upto, hs], ((1,), (1,)))
            t_ids = lax.broadcasted_iota(jnp.int32, (tb, upto), 0) + b * tb
            s_ids = lax.broadcasted_iota(jnp.int32, (tb, upto), 1)
            low = jnp.broadcast_to(lo_ref[ts, 0:1], (tb, upto))
            allowed = (s_ids <= t_ids) & (s_ids >= low)
            scores = jnp.where(allowed, scores, 0.0).astype(BF16)
            within[h, ts, :] = dot(scores, v_ref[:upto, hs])

    attend(0)
    within_0[...] = within[0].astype(BF16)
    near_send(2)

    def p2_copy(h, k, i):
        return remote(
            r_in.at[h, i], r_in.at[h, i], p2s.at[h, k], p2r.at[h, k], z_dev((z + k) % nz))

    others = pl.ds(0, row - 1)
    for h in range(heads):
        wait_bytes(s_in.at[h, others], p1r.at[h])
        row_sum = functools.reduce(
            jnp.add, [w_row_sum[j] * s_in[h, j].astype(F32) for j in range(row)])
        r_in[h, z] = row_sum.astype(BF16)
        for k in far_first(nz):
            @pl.when(z + k < nz)
            def _():
                p2_copy(h, k, z).start()

    w_own = {
        (i, j): flag((first + j + 1) * tok > row_start[i]) for i in range(row) for j in range(i)}
    for h in range(heads):
        state = [s_in[h, j].astype(F32) for j in range(row)]
        for i in range(row):
            total = jnp.zeros((sl, DH), F32)
            for j in range(i):
                total = total + w_own[i, j] * state[j]
            crow[h, i] = total
    attend(1)

    for h in range(heads):
        for k in range(1, nz):
            @pl.when(z >= k)
            def _():
                p2_copy(h, k, (z + nz - k) % nz).wait_recv()
        past = functools.reduce(
            jnp.add, [w_rows[i] * r_in[h, i].astype(F32) for i in range(nz)])
        for i in range(row):
            c_out[h, i] = (crow[h, i] + w_past[i] * past).astype(BF16)
        for k in far_first(row):
            i = (r + k) % row
            remote(c_out.at[h, i], c_in.at[h, part(r)], p3s.at[h], p3r.at[h], row_dev(i)).start()
        c_in[h, part(r), :] = c_out[h, r]

    attend(2)

    def z_block(i, first, count):
        return wcol.at[pl.ds(first, count), pl.ds(pl.multiple_of(i * wr, 16), wr), :]

    def z_copy(way, d, half, starting):
        step = 1 if way == 0 else nz - 1
        away = d if starting else d + 1
        owner = (z + away * (nz - step)) % nz
        count = yh // 2 if half == 0 else yh - yh // 2
        block = z_block(owner, first_rel + half * (yh // 2), count)
        return block, block, wzs.at[way, half, d], wzr.at[way, half, d], z_dev((z + step) % nz)

    own_rels, twin_rels = 1 + yh * c, 1 + yh * (1 - c)
    twin = row_dev(x * 2 + (1 - c))

    def to_twin(i):
        block = z_block(i, own_rels, yh - 1)
        remote(block, block, wcs, wcr, twin).start()

    def z_step(d, half):
        for way in range(2):
            if d > 0 and (d < zh or way == half):
                remote(*z_copy(way, d - 1, half, False)).wait_recv()
        for way in range(2):
            if d < zh - 1 or (d == zh - 1 and way == half):
                send(*z_copy(way, d, half, True))
        if half == 1:
            to_twin((z + d) % nz)
            if 0 < d < zh:
                to_twin((z + nz - d) % nz)

    def y_copy(way, d, h, starting):
        slot = (ny - d) % ny if way == 0 else d
        later = ny - d - 1 if way == 0 else d + 1
        ts = pl.ds(0, tok)
        if d == yh - 1:
            ts = pl.ds(way * tb, tb)
        src, dst = norm_all.at[slot, h, ts], norm_all.at[later, h, ts]
        to = (y + 1) % ny if way == 0 else (y + ny - 1) % ny
        return src, dst, ys.at[way, d, h], yr.at[way, d, h], y_dev(to)

    def y_send(d, h):
        for way in range(2):
            send(*y_copy(way, d, h, True))

    def y_wait(d, h, ways=(0, 1)):
        for way in ways:
            remote(*y_copy(way, d - 1, h, False)).wait_recv()

    def norm(dst, query, inside, carried, scale):
        for b in range(2):
            ts = slice(b * tb, (b + 1) * tb)
            term = dot(query(ts), carried)
            mixture = inside(ts).astype(F32) + jnp.where(lo_ref[ts, :] < 0, term, 0.0)
            square_mean = jnp.mean(mixture * mixture, axis=-1, keepdims=True)
            gains = jnp.broadcast_to(scale[None, :], (tb, DH))
            dst[ts, :] = (mixture * lax.rsqrt(square_mean + 1e-06) * gains).astype(BF16)

    for h in range(heads):
        hs = slice(h * DH, (h + 1) * DH)
        wait_bytes(c_in.at[h, pl.ds(0, sl * (row - 1))], p3r.at[h])
        if h == 0:
            near_send(3)
        norm(norm_all.at[0, h], lambda ts: q_ref[ts, hs], lambda ts: within[h, ts, :], c_in[h], gain[hs])
        if h > 0:
            y_send(0, h)

    def project(rel, start=False):
        for b in range(2):
            ts = slice(b * tb, (b + 1) * tb)
            left = jnp.concatenate([norm_all[rel, h, ts, :] for h in range(heads)], axis=1)
            term = dot(left, wcol[rel])
            acc[ts, :] = term if start else acc[ts, :] + term

    def y_step(d, h):
        if d == 1 and h == 0:
            for way in range(2):
                for kind in range(4):
                    near_copy(way, kind).wait_recv()
                norm(
                    norm_all.at[ny - 1 if way == 0 else 1, 0], lambda ts: q_near[way, ts, :],
                    lambda ts: in_near[way, ts, :], c_near[way], g_near[way][0:DH])
        else:
            y_wait(d, h)
        y_send(d, h)

    loads[3].wait()
    project(0, True)
    wait_bytes(z_block(z, first_rel, yh), wyr)
    z_step(0, 0)
    z_step(0, 1)
    def side(e, core):
        return e + core * (ny - 2 * e)

    y_events = [(d, h) for d in range(1, yh) for h in range(heads)]
    z_events = [(d, half) for d in range(1, zh + 1) for half in range(2)]
    z_after = [min(m + 1, len(y_events) - 2) for m in range(len(z_events))]
    for n, (d, h) in enumerate(y_events):
        y_step(d, h)
        for after, event in zip(z_after, z_events):
            if after == n:
                z_step(*event)
        if n == 2:
            for h2 in range(heads):
                wait_bytes(s_in.at[h2, others], p1s.at[h2])
                wait_bytes(s_in.at[h2, others], p3s.at[h2])
                for k in range(1, nz):
                    @pl.when(z + k < nz)
                    def _():
                        p2_copy(h2, k, z).wait_send()
            wait_bytes(z_block(z, first_rel, yh), wys)
        if n == len(y_events) // 2:
            early = len(sends)
        if n == len(y_events) - 2:
            for e in range(1, yh - 1):
                project(side(e, c))
        if n == len(y_events) - 1:
            project(side(yh - 1, c))
            wait_bytes(wcol.at[pl.ds(twin_rels, yh - 1)], wcr)
            wait_bytes(wcol.at[pl.ds(own_rels, yh - 1)], wcs)
            for copy in sends[:early]:
                copy.wait_send()
            for e in range(1, yh):
                project(side(e, 1 - c))
    for h in range(heads):
        hs = slice(h * DH, (h + 1) * DH)
        for way in range(2):
            ts = slice(way * tb, (way + 1) * tb)
            y_wait(yh, h, (way,))
            total = acc[ts, :] + dot(norm_all[yh, h, ts, :], wcol[yh, hs, :])
            if h < heads - 1:
                acc[ts, :] = total
            else:
                out_v[ts, :] = total.astype(BF16)
    for way in range(2):
        for kind in range(4):
            near_copy(way, kind).wait_send()
    for copy in sends[early:]:
        copy.wait_send()


def body(nz, row, ny, queries, key_vectors, value_vectors, doc_lengths, norm_gain, out_weight):
    tok, width = queries.shape
    heads = width // DH
    cols = out_weight.shape[1] // ny
    yh, zh = ny // 2, nz // 2
    sl = DH // row
    dma = pltpu.SemaphoreType.DMA
    any_spec = pl.BlockSpec(memory_space=pl.ANY)
    return pl.pallas_call(
        functools.partial(layer_kernel, nz, row, ny),
        name="layer",
        out_shape=pltpu.VMEM((tok, cols), BF16),
        in_specs=[any_spec] * 6,
        out_specs=pl.BlockSpec(memory_space=pltpu.VMEM),
        scratch_shapes=[
            pltpu.SMEM(doc_lengths.shape, jnp.int32),
            pltpu.VMEM((width,), F32),
            pltpu.VMEM((tok, width), BF16),
            pltpu.VMEM((tok, width), BF16),
            pltpu.VMEM((tok, width), BF16),
            pltpu.VMEM((heads, DH, DH), BF16),
            pltpu.VMEM((heads, row, sl, DH), BF16),
            pltpu.VMEM((heads, nz, sl, DH), BF16),
            pltpu.VMEM((heads, row, sl, DH), F32),
            pltpu.VMEM((heads, row, sl, DH), BF16),
            pltpu.VMEM((heads, DH, DH), BF16),
            pltpu.VMEM((tok, DH), jnp.int32),
            pltpu.VMEM((heads, tok, DH), F32),
            pltpu.VMEM((tok, DH), BF16),
            pltpu.VMEM((2, tok, DH), BF16),
            pltpu.VMEM((2, tok, DH), BF16),
            pltpu.VMEM((2, DH, DH), BF16),
            pltpu.VMEM((width,), F32),
            pltpu.VMEM((width,), F32),
            pltpu.VMEM((ny, heads, tok, DH), BF16),
            pltpu.VMEM((ny, width, cols), BF16),
            pltpu.VMEM((tok, cols), F32),
            dma((6,)),
            dma((heads,)), dma((heads,)),
            dma((heads, nz)), dma((heads, nz)),
            dma((heads,)), dma((heads,)),
            dma(()), dma(()),
            dma((2, 2, zh)), dma((2, 2, zh)),
            dma(()), dma(()),
            dma((2, yh, heads)), dma((2, yh, heads)),
            dma((2, 4)), dma((2, 4)),
        ],
        compiler_params=pltpu.CompilerParams(collective_id=0, has_side_effects=True),
    )(queries, key_vectors, value_vectors, doc_lengths, norm_gain, out_weight)


def solution(mesh, row=ROW):
    nz, ny = mesh.shape["seq"] // row, mesh.shape["head"]
    return jax.shard_map(
        functools.partial(body, nz, row, ny),
        mesh=mesh,
        in_specs=(
            P("seq", "head"),
            P("seq", "head"),
            P("seq", "head"),
            P(),
            P("head"),
            P("head", None),
        ),
        out_specs=P("seq", "head"),
        check_vma=False,
    )
```

```python
import functools

import jax
import jax.numpy as jnp
from jax import lax
from jax.experimental import pallas as pl
from jax.experimental.pallas import tpu as pltpu
from jax.sharding import PartitionSpec as P

DH = 128
ROW = 8
MESH = pl.DeviceIdType.MESH
F32 = jnp.float32
BF16 = jnp.bfloat16


def dot(a, b, dims=((1,), (0,))):
    return lax.dot_general(a, b, (dims, ((), ())), preferred_element_type=F32)


def layer_kernel(
    nz, row, ny,
    q_any, k_any, v_any, lens_any, gain_any, w_any, out_v,
    lens, gain, q_ref, k_ref, v_ref, s_loc, s_in, r_in, crow, c_out, c_in, lo_ref, within, within_0, q_near, in_near, c_near, g_below, g_above, norm_all, wcol, acc,
    load_sem, p1s, p1r, p2s, p2r, p3s, p3r, wys, wyr, wzs, wzr, wcs, wcr, ys, yr, es, er, later, level,
):
    tok, width = q_ref.shape
    heads = width // DH
    cols = out_v.shape[1]
    yh, zh = ny // 2, nz // 2
    sl = DH // row
    wr = width // nz
    seq, y = lax.axis_index("seq"), lax.axis_index("head")
    z, r = seq // row, seq % row
    x, c = r // 2, r % 2
    sends = []

    def remote(src, dst, ssem, rsem, target):
        return pltpu.make_async_remote_copy(
            src_ref=src, dst_ref=dst, send_sem=ssem, recv_sem=rsem,
            device_id=target, device_id_type=MESH)

    def send(*args):
        copy = remote(*args)
        copy.start()
        sends.append(copy)

    def wait_bytes(ref, sem):
        pltpu.make_async_copy(ref, ref, sem).wait()

    def row_dev(i):
        return (z * row + i, y)

    def z_dev(i):
        return (i * row + r, y)

    def y_dev(i):
        return (seq, i)

    barrier = pltpu.get_barrier_semaphore()
    def far_first(n):
        return sorted(range(1, n), key=lambda k: -min(k, n - k))

    y_near = (y_dev((y + 1) % ny), y_dev((y + ny - 1) % ny))
    peers = list(y_near) + [row_dev((r + k) % row) for k in far_first(row)]
    r_in[...] = jnp.zeros_like(r_in)
    for k in range(nz - 1, 0, -1):
        @pl.when(z + k < nz)
        def _():
            pl.semaphore_signal(barrier, inc=1, device_id=z_dev((z + k) % nz), device_id_type=MESH)
    for peer in peers:
        pl.semaphore_signal(barrier, inc=1, device_id=peer, device_id_type=MESH)

    small = [
        pltpu.make_async_copy(lens_any, lens, load_sem.at[4]),
        pltpu.make_async_copy(gain_any, gain, load_sem.at[5]),
    ]
    loads = [
        pltpu.make_async_copy(k_any, k_ref, load_sem.at[0]),
        pltpu.make_async_copy(v_any, v_ref, load_sem.at[1]),
        pltpu.make_async_copy(q_any, q_ref, load_sem.at[2]),
        pltpu.make_async_copy(
            w_any.at[:, pl.ds(pl.multiple_of(y * cols, 128), cols)], wcol.at[0], load_sem.at[3]),
    ]
    for load in small[:1] + loads + small[1:]:
        load.start()

    small[0].wait()
    bounds, total = [], jnp.int32(0)
    for d in range(lens.shape[0]):
        total = total + lens[d]
        bounds.append(total)

    def start_of(position):
        found = jnp.int32(0)
        for bound in bounds:
            found = jnp.where(bound <= position, bound, found)
        return found

    def flag(condition):
        return jnp.where(condition, jnp.float32(1), jnp.float32(0))

    offset = seq * tok
    lo_last = start_of(offset + (tok - 1)) - offset
    first = z * row
    row_start = [start_of((first + i) * tok) for i in range(row)]
    next_start = start_of((first + row) * tok)
    w_row_sum = [flag((first + j + 1) * tok > next_start) for j in range(row)]
    w_past = [flag(row_start[i] < first * tok) for i in range(row)]
    w_rows = [flag(((i + 1) * row * tok > row_start[0]) & (i < z)) for i in range(nz)]

    rows = lax.broadcasted_iota(jnp.int32, (tok, DH), 0)
    keep = flag(rows >= lo_last)
    loads[0].wait()
    loads[1].wait()
    for h in range(heads):
        hs = slice(h * DH, (h + 1) * DH)
        key = (k_ref[:, hs].astype(F32) * keep).astype(BF16)
        s_loc[h] = dot(key, v_ref[:, hs], ((0,), (0,))).astype(BF16)

    pl.semaphore_wait(barrier, len(peers) + z)
    for k in range(nz - 1, 0, -1):
        @pl.when(z >= k)
        def _():
            pl.semaphore_signal(later, inc=1, device_id=z_dev((z + nz - k) % nz), device_id_type=MESH)

    def relay(n):
        if n > 0:
            pl.semaphore_wait(level.at[n - 1], 2)
        if n < yh - 1:
            for peer in y_near:
                pl.semaphore_signal(level.at[n], inc=1, device_id=peer, device_id_type=MESH)

    relay(0)

    def part(i):
        return pl.ds(pl.multiple_of(i * sl, 16), sl)

    for h in range(heads):
        for k in far_first(row):
            i = (r + k) % row
            remote(s_loc.at[h, part(i)], s_in.at[h, r], p1s.at[h], p1r.at[h], row_dev(i)).start()

    g_near = (g_below, g_above)

    def near_copy(way, kind):
        src, dst = (
            (q_ref.at[:, pl.ds(0, DH)], q_near.at[way]),
            (gain, g_near[way]),
            (within_0, in_near.at[way]),
            (c_in.at[0], c_near.at[way]),
        )[kind]
        return remote(src, dst, es.at[way, kind], er.at[way, kind], y_near[way])

    def near_send(kind):
        for way in range(2):
            near_copy(way, kind).start()

    loads[2].wait()
    near_send(0)
    small[1].wait()
    near_send(1)

    first_rel = 1 + (yh - 1) * c
    z_rows = pl.ds(pl.multiple_of(z * wr, 16), wr)
    for h in range(heads):
        s_in[h, r] = s_loc[h, part(r), :]
    lo = jnp.zeros((tok, DH), jnp.int32) - offset
    for bound in bounds:
        lo = jnp.where(rows >= bound - offset, bound - offset, lo)
    lo_ref[...] = lo

    tb = tok // 2

    def attend(h):
        hs = slice(h * DH, (h + 1) * DH)
        for b in range(2):
            upto = (b + 1) * tb
            ts = slice(b * tb, upto)
            scores = dot(q_ref[ts, hs], k_ref[:upto, hs], ((1,), (1,)))
            t_ids = lax.broadcasted_iota(jnp.int32, (tb, upto), 0) + b * tb
            s_ids = lax.broadcasted_iota(jnp.int32, (tb, upto), 1)
            low = jnp.broadcast_to(lo_ref[ts, 0:1], (tb, upto))
            allowed = (s_ids <= t_ids) & (s_ids >= low)
            scores = jnp.where(allowed, scores, 0.0).astype(BF16)
            within[h, ts, :] = dot(scores, v_ref[:upto, hs])

    attend(0)
    within_0[...] = within[0].astype(BF16)
    near_send(2)

    relay(1)
    def p2_copy(h, k, i):
        return remote(
            r_in.at[h, i], r_in.at[h, i], p2s.at[h, k], p2r.at[h, k], z_dev((z + k) % nz))

    others = pl.ds(0, row - 1)
    for h in range(heads):
        wait_bytes(s_in.at[h, others], p1r.at[h])
        row_sum = functools.reduce(
            jnp.add, [w_row_sum[j] * s_in[h, j].astype(F32) for j in range(row)])
        r_in[h, z] = row_sum.astype(BF16)
        if h == 0:
            @pl.when(z < nz - 1)
            def _():
                pl.semaphore_wait(later, nz - 1 - z)
        for k in far_first(nz):
            @pl.when(z + k < nz)
            def _():
                p2_copy(h, k, z).start()

    w_own = {
        (i, j): flag((first + j + 1) * tok > row_start[i]) for i in range(row) for j in range(i)}
    for h in range(heads):
        state = [s_in[h, j].astype(F32) for j in range(row)]
        for i in range(row):
            total = jnp.zeros((sl, DH), F32)
            for j in range(i):
                total = total + w_own[i, j] * state[j]
            crow[h, i] = total
    attend(1)

    for n in range(2, yh):
        relay(n)
    for i in range(yh):
        rel = yh + i * (2 * c - 1)
        plane = (y + ny - rel) % ny
        remote(
            w_any.at[z_rows, pl.ds(pl.multiple_of(plane * cols, 128), cols)],
            wcol.at[rel, z_rows, :], wys, wyr, y_dev(plane)).start()
    for h in range(heads):
        for k in range(1, nz):
            @pl.when(z >= k)
            def _():
                p2_copy(h, k, (z + nz - k) % nz).wait_recv()
        past = functools.reduce(
            jnp.add, [w_rows[i] * r_in[h, i].astype(F32) for i in range(nz)])
        for i in range(row):
            c_out[h, i] = (crow[h, i] + w_past[i] * past).astype(BF16)
        for k in far_first(row):
            i = (r + k) % row
            remote(c_out.at[h, i], c_in.at[h, part(r)], p3s.at[h], p3r.at[h], row_dev(i)).start()
        c_in[h, part(r), :] = c_out[h, r]

    attend(2)

    def z_block(i, first, count):
        return wcol.at[pl.ds(first, count), pl.ds(pl.multiple_of(i * wr, 16), wr), :]

    def z_copy(way, d, half, starting):
        step = 1 if way == 0 else nz - 1
        away = d if starting else d + 1
        owner = (z + away * (nz - step)) % nz
        count = yh // 2 if half == 0 else yh - yh // 2
        block = z_block(owner, first_rel + half * (yh // 2), count)
        return block, block, wzs.at[way, half, d], wzr.at[way, half, d], z_dev((z + step) % nz)

    own_rels, twin_rels = 1 + yh * c, 1 + yh * (1 - c)
    twin = row_dev(x * 2 + (1 - c))

    def to_twin(i):
        block = z_block(i, own_rels, yh - 1)
        remote(block, block, wcs, wcr, twin).start()

    def z_step(d, half):
        for way in range(2):
            if d > 0 and (d < zh or way == half):
                remote(*z_copy(way, d - 1, half, False)).wait_recv()
        for way in range(2):
            if d < zh - 1 or (d == zh - 1 and way == half):
                send(*z_copy(way, d, half, True))
        if half == 1:
            to_twin((z + d) % nz)
            if 0 < d < zh:
                to_twin((z + nz - d) % nz)

    def y_copy(way, d, h, starting):
        slot = (ny - d) % ny if way == 0 else d
        later = ny - d - 1 if way == 0 else d + 1
        ts = pl.ds(0, tok)
        if d == yh - 1:
            ts = pl.ds(way * tb, tb)
        src, dst = norm_all.at[slot, h, ts], norm_all.at[later, h, ts]
        to = (y + 1) % ny if way == 0 else (y + ny - 1) % ny
        return src, dst, ys.at[way, d, h], yr.at[way, d, h], y_dev(to)

    def y_send(d, h):
        for way in range(2):
            send(*y_copy(way, d, h, True))

    def y_wait(d, h, ways=(0, 1)):
        for way in ways:
            remote(*y_copy(way, d - 1, h, False)).wait_recv()

    def norm(dst, query, inside, carried, scale):
        for b in range(2):
            ts = slice(b * tb, (b + 1) * tb)
            term = dot(query(ts), carried)
            mixture = inside(ts).astype(F32) + jnp.where(lo_ref[ts, :] < 0, term, 0.0)
            square_mean = jnp.mean(mixture * mixture, axis=-1, keepdims=True)
            gains = jnp.broadcast_to(scale[None, :], (tb, DH))
            dst[ts, :] = (mixture * lax.rsqrt(square_mean + 1e-06) * gains).astype(BF16)

    for h in range(heads):
        hs = slice(h * DH, (h + 1) * DH)
        wait_bytes(c_in.at[h, pl.ds(0, sl * (row - 1))], p3r.at[h])
        if h == 0:
            near_send(3)
        norm(norm_all.at[0, h], lambda ts: q_ref[ts, hs], lambda ts: within[h, ts, :], c_in[h], gain[hs])
        if h > 0:
            y_send(0, h)

    def project(rel, start=False):
        for b in range(2):
            ts = slice(b * tb, (b + 1) * tb)
            left = jnp.concatenate([norm_all[rel, h, ts, :] for h in range(heads)], axis=1)
            term = dot(left, wcol[rel])
            acc[ts, :] = term if start else acc[ts, :] + term

    def y_step(d, h):
        if d == 1 and h == 0:
            for way in range(2):
                for kind in range(4):
                    near_copy(way, kind).wait_recv()
                norm(
                    norm_all.at[ny - 1 if way == 0 else 1, 0], lambda ts: q_near[way, ts, :],
                    lambda ts: in_near[way, ts, :], c_near[way], g_near[way][0:DH])
        else:
            y_wait(d, h)
        y_send(d, h)

    loads[3].wait()
    project(0, True)
    wait_bytes(z_block(z, first_rel, yh), wyr)
    z_step(0, 0)
    z_step(0, 1)
    def side(e, core):
        return e + core * (ny - 2 * e)

    y_events = [(d, h) for d in range(1, yh) for h in range(heads)]
    z_events = [(d, half) for d in range(1, zh + 1) for half in range(2)]
    z_after = [min(m + 1, len(y_events) - 2) for m in range(len(z_events))]
    for n, (d, h) in enumerate(y_events):
        y_step(d, h)
        for after, event in zip(z_after, z_events):
            if after == n:
                z_step(*event)
        if n == 2:
            for h2 in range(heads):
                wait_bytes(s_in.at[h2, others], p1s.at[h2])
                wait_bytes(s_in.at[h2, others], p3s.at[h2])
                for k in range(1, nz):
                    @pl.when(z + k < nz)
                    def _():
                        p2_copy(h2, k, z).wait_send()
            wait_bytes(z_block(z, first_rel, yh), wys)
        if n == len(y_events) // 2:
            early = len(sends)
        if n == len(y_events) - 2:
            for e in range(1, yh - 1):
                project(side(e, c))
        if n == len(y_events) - 1:
            project(side(yh - 1, c))
            wait_bytes(wcol.at[pl.ds(twin_rels, yh - 1)], wcr)
            wait_bytes(wcol.at[pl.ds(own_rels, yh - 1)], wcs)
            for copy in sends[:early]:
                copy.wait_send()
            for e in range(1, yh):
                project(side(e, 1 - c))
    for h in range(heads):
        hs = slice(h * DH, (h + 1) * DH)
        for way in range(2):
            ts = slice(way * tb, (way + 1) * tb)
            y_wait(yh, h, (way,))
            total = acc[ts, :] + dot(norm_all[yh, h, ts, :], wcol[yh, hs, :])
            if h < heads - 1:
                acc[ts, :] = total
            else:
                out_v[ts, :] = total.astype(BF16)
    for way in range(2):
        for kind in range(4):
            near_copy(way, kind).wait_send()
    for copy in sends[early:]:
        copy.wait_send()


def body(nz, row, ny, queries, key_vectors, value_vectors, doc_lengths, norm_gain, out_weight):
    tok, width = queries.shape
    heads = width // DH
    cols = out_weight.shape[1] // ny
    yh, zh = ny // 2, nz // 2
    sl = DH // row
    dma = pltpu.SemaphoreType.DMA
    any_spec = pl.BlockSpec(memory_space=pl.ANY)
    return pl.pallas_call(
        functools.partial(layer_kernel, nz, row, ny),
        name="layer",
        out_shape=pltpu.VMEM((tok, cols), BF16),
        in_specs=[any_spec] * 6,
        out_specs=pl.BlockSpec(memory_space=pltpu.VMEM),
        scratch_shapes=[
            pltpu.SMEM(doc_lengths.shape, jnp.int32),
            pltpu.VMEM((width,), F32),
            pltpu.VMEM((tok, width), BF16),
            pltpu.VMEM((tok, width), BF16),
            pltpu.VMEM((tok, width), BF16),
            pltpu.VMEM((heads, DH, DH), BF16),
            pltpu.VMEM((heads, row, sl, DH), BF16),
            pltpu.VMEM((heads, nz, sl, DH), BF16),
            pltpu.VMEM((heads, row, sl, DH), F32),
            pltpu.VMEM((heads, row, sl, DH), BF16),
            pltpu.VMEM((heads, DH, DH), BF16),
            pltpu.VMEM((tok, DH), jnp.int32),
            pltpu.VMEM((heads, tok, DH), F32),
            pltpu.VMEM((tok, DH), BF16),
            pltpu.VMEM((2, tok, DH), BF16),
            pltpu.VMEM((2, tok, DH), BF16),
            pltpu.VMEM((2, DH, DH), BF16),
            pltpu.VMEM((width,), F32),
            pltpu.VMEM((width,), F32),
            pltpu.VMEM((ny, heads, tok, DH), BF16),
            pltpu.VMEM((ny, width, cols), BF16),
            pltpu.VMEM((tok, cols), F32),
            dma((6,)),
            dma((heads,)), dma((heads,)),
            dma((heads, nz)), dma((heads, nz)),
            dma((heads,)), dma((heads,)),
            dma(()), dma(()),
            dma((2, 2, zh)), dma((2, 2, zh)),
            dma(()), dma(()),
            dma((2, yh, heads)), dma((2, yh, heads)),
            dma((2, 4)), dma((2, 4)),
            pltpu.SemaphoreType.REGULAR,
            pltpu.SemaphoreType.REGULAR((yh - 1,)),
        ],
        compiler_params=pltpu.CompilerParams(collective_id=0, has_side_effects=True),
    )(queries, key_vectors, value_vectors, doc_lengths, norm_gain, out_weight)


def solution(mesh, row=ROW):
    nz, ny = mesh.shape["seq"] // row, mesh.shape["head"]
    return jax.shard_map(
        functools.partial(body, nz, row, ny),
        mesh=mesh,
        in_specs=(
            P("seq", "head"),
            P("seq", "head"),
            P("seq", "head"),
            P(),
            P("head"),
            P("head", None),
        ),
        out_specs=P("seq", "head"),
        check_vma=False,
    )
```

```python
import functools

import jax
import jax.numpy as jnp
from jax import lax
from jax.experimental import pallas as pl
from jax.experimental.pallas import tpu as pltpu
from jax.sharding import PartitionSpec as P

DH = 128
ROW = 8
MESH = pl.DeviceIdType.MESH
F32 = jnp.float32
BF16 = jnp.bfloat16


def dot(a, b, dims=((1,), (0,))):
    return lax.dot_general(a, b, (dims, ((), ())), preferred_element_type=F32)


def layer_kernel(
    nz, row, ny,
    q_any, k_any, v_any, lens_any, gain_any, w_any, out_v,
    lens, gain, q_ref, k_ref, v_ref, s_loc, s_in, r_in, crow, c_out, c_in, lo_ref, within, within_0, q_near, in_near, c_near, g_below, g_above, norm_all, wcol, acc,
    load_sem, p1s, p1r, p2s, p2r, p3s, p3r, wys, wyr, wzs, wzr, wcs, wcr, ys, yr, es, er, later, level,
):
    tok, width = q_ref.shape
    heads = width // DH
    cols = out_v.shape[1]
    yh, zh = ny // 2, nz // 2
    sl = DH // row
    wr = width // nz
    seq, y = lax.axis_index("seq"), lax.axis_index("head")
    z, r = seq // row, seq % row
    x, c = r // 2, r % 2
    sends = []

    def remote(src, dst, ssem, rsem, target):
        return pltpu.make_async_remote_copy(
            src_ref=src, dst_ref=dst, send_sem=ssem, recv_sem=rsem,
            device_id=target, device_id_type=MESH)

    def send(*args):
        copy = remote(*args)
        copy.start()
        sends.append(copy)

    def wait_bytes(ref, sem):
        pltpu.make_async_copy(ref, ref, sem).wait()

    def row_dev(i):
        return (z * row + i, y)

    def z_dev(i):
        return (i * row + r, y)

    def y_dev(i):
        return (seq, i)

    barrier = pltpu.get_barrier_semaphore()
    def far_first(n):
        return sorted(range(1, n), key=lambda k: -min(k, n - k))

    y_near = (y_dev((y + 1) % ny), y_dev((y + ny - 1) % ny))
    peers = list(y_near) + [row_dev((r + k) % row) for k in far_first(row)]
    r_in[...] = jnp.zeros_like(r_in)
    for k in range(nz - 1, 0, -1):
        @pl.when(z + k < nz)
        def _():
            pl.semaphore_signal(barrier, inc=1, device_id=z_dev((z + k) % nz), device_id_type=MESH)
    for peer in peers:
        pl.semaphore_signal(barrier, inc=1, device_id=peer, device_id_type=MESH)

    small = [
        pltpu.make_async_copy(lens_any, lens, load_sem.at[4]),
        pltpu.make_async_copy(gain_any, gain, load_sem.at[5]),
    ]
    loads = [
        pltpu.make_async_copy(k_any, k_ref, load_sem.at[0]),
        pltpu.make_async_copy(v_any, v_ref, load_sem.at[1]),
        pltpu.make_async_copy(q_any, q_ref, load_sem.at[2]),
        pltpu.make_async_copy(
            w_any.at[:, pl.ds(pl.multiple_of(y * cols, 128), cols)], wcol.at[0], load_sem.at[3]),
    ]
    for load in small[:1] + loads + small[1:]:
        load.start()

    small[0].wait()
    bounds, total = [], jnp.int32(0)
    for d in range(lens.shape[0]):
        total = total + lens[d]
        bounds.append(total)

    def start_of(position):
        found = jnp.int32(0)
        for bound in bounds:
            found = jnp.where(bound <= position, bound, found)
        return found

    def flag(condition):
        return jnp.where(condition, jnp.float32(1), jnp.float32(0))

    offset = seq * tok
    lo_last = start_of(offset + (tok - 1)) - offset
    first = z * row
    row_start = [start_of((first + i) * tok) for i in range(row)]
    next_start = start_of((first + row) * tok)
    w_row_sum = [flag((first + j + 1) * tok > next_start) for j in range(row)]
    w_past = [flag(row_start[i] < first * tok) for i in range(row)]
    w_rows = [flag(((i + 1) * row * tok > row_start[0]) & (i < z)) for i in range(nz)]

    rows = lax.broadcasted_iota(jnp.int32, (tok, DH), 0)
    keep = flag(rows >= lo_last)
    loads[0].wait()
    loads[1].wait()
    for h in range(heads):
        hs = slice(h * DH, (h + 1) * DH)
        key = (k_ref[:, hs].astype(F32) * keep).astype(BF16)
        s_loc[h] = dot(key, v_ref[:, hs], ((0,), (0,))).astype(BF16)

    pl.semaphore_wait(barrier, len(peers) + z)
    for k in range(nz - 1, 0, -1):
        @pl.when(z >= k)
        def _():
            pl.semaphore_signal(later, inc=1, device_id=z_dev((z + nz - k) % nz), device_id_type=MESH)

    def relay(n):
        if n > 0:
            pl.semaphore_wait(level.at[n - 1], 2)
        if n < yh - 1:
            for peer in y_near:
                pl.semaphore_signal(level.at[n], inc=1, device_id=peer, device_id_type=MESH)

    relay(0)

    def part(i):
        return pl.ds(pl.multiple_of(i * sl, 16), sl)

    for h in range(heads):
        for k in far_first(row):
            i = (r + k) % row
            remote(s_loc.at[h, part(i)], s_in.at[h, r], p1s.at[h], p1r.at[h], row_dev(i)).start()

    g_near = (g_below, g_above)

    def near_copy(way, kind):
        src, dst = (
            (q_ref.at[:, pl.ds(0, DH)], q_near.at[way]),
            (gain, g_near[way]),
            (within_0, in_near.at[way]),
            (c_in.at[0], c_near.at[way]),
        )[kind]
        return remote(src, dst, es.at[way, kind], er.at[way, kind], y_near[way])

    def near_send(kind):
        for way in range(2):
            near_copy(way, kind).start()

    loads[2].wait()
    near_send(0)
    small[1].wait()
    near_send(1)

    first_rel = 1 + (yh - 1) * c
    z_rows = pl.ds(pl.multiple_of(z * wr, 16), wr)
    for h in range(heads):
        s_in[h, r] = s_loc[h, part(r), :]
    lo = jnp.zeros((tok, DH), jnp.int32) - offset
    for bound in bounds:
        lo = jnp.where(rows >= bound - offset, bound - offset, lo)
    lo_ref[...] = lo

    tb = tok // 2

    def attend(h):
        hs = slice(h * DH, (h + 1) * DH)
        for b in range(2):
            upto = (b + 1) * tb
            ts = slice(b * tb, upto)
            scores = dot(q_ref[ts, hs], k_ref[:upto, hs], ((1,), (1,)))
            t_ids = lax.broadcasted_iota(jnp.int32, (tb, upto), 0) + b * tb
            s_ids = lax.broadcasted_iota(jnp.int32, (tb, upto), 1)
            low = jnp.broadcast_to(lo_ref[ts, 0:1], (tb, upto))
            allowed = (s_ids <= t_ids) & (s_ids >= low)
            scores = jnp.where(allowed, scores, 0.0).astype(BF16)
            within[h, ts, :] = dot(scores, v_ref[:upto, hs])

    relay(1)
    attend(0)
    within_0[...] = within[0].astype(BF16)
    near_send(2)

    relay(2)
    def p2_copy(h, k, i):
        return remote(
            r_in.at[h, i], r_in.at[h, i], p2s.at[h, k], p2r.at[h, k], z_dev((z + k) % nz))

    others = pl.ds(0, row - 1)
    for h in range(heads):
        wait_bytes(s_in.at[h, others], p1r.at[h])
        row_sum = functools.reduce(
            jnp.add, [w_row_sum[j] * s_in[h, j].astype(F32) for j in range(row)])
        r_in[h, z] = row_sum.astype(BF16)
        if h == 0:
            @pl.when(z < nz - 1)
            def _():
                pl.semaphore_wait(later, nz - 1 - z)
        for k in far_first(nz):
            @pl.when(z + k < nz)
            def _():
                p2_copy(h, k, z).start()

    w_own = {
        (i, j): flag((first + j + 1) * tok > row_start[i]) for i in range(row) for j in range(i)}
    for h in range(heads):
        state = [s_in[h, j].astype(F32) for j in range(row)]
        for i in range(row):
            total = jnp.zeros((sl, DH), F32)
            for j in range(i):
                total = total + w_own[i, j] * state[j]
            crow[h, i] = total
    attend(1)

    for n in range(3, yh):
        relay(n)
    for i in range(yh):
        rel = yh + i * (2 * c - 1)
        plane = (y + ny - rel) % ny
        remote(
            w_any.at[z_rows, pl.ds(pl.multiple_of(plane * cols, 128), cols)],
            wcol.at[rel, z_rows, :], wys, wyr, y_dev(plane)).start()
    for h in range(heads):
        for k in range(1, nz):
            @pl.when(z >= k)
            def _():
                p2_copy(h, k, (z + nz - k) % nz).wait_recv()
        past = functools.reduce(
            jnp.add, [w_rows[i] * r_in[h, i].astype(F32) for i in range(nz)])
        for i in range(row):
            c_out[h, i] = (crow[h, i] + w_past[i] * past).astype(BF16)
        for k in far_first(row):
            i = (r + k) % row
            remote(c_out.at[h, i], c_in.at[h, part(r)], p3s.at[h], p3r.at[h], row_dev(i)).start()
        c_in[h, part(r), :] = c_out[h, r]

    attend(2)

    def z_block(i, first, count):
        return wcol.at[pl.ds(first, count), pl.ds(pl.multiple_of(i * wr, 16), wr), :]

    def z_copy(way, d, half, starting):
        step = 1 if way == 0 else nz - 1
        away = d if starting else d + 1
        owner = (z + away * (nz - step)) % nz
        count = yh // 2 if half == 0 else yh - yh // 2
        block = z_block(owner, first_rel + half * (yh // 2), count)
        return block, block, wzs.at[way, half, d], wzr.at[way, half, d], z_dev((z + step) % nz)

    own_rels, twin_rels = 1 + yh * c, 1 + yh * (1 - c)
    twin = row_dev(x * 2 + (1 - c))

    def to_twin(i):
        block = z_block(i, own_rels, yh - 1)
        remote(block, block, wcs, wcr, twin).start()

    def z_step(d, half):
        for way in range(2):
            if d > 0 and (d < zh or way == half):
                remote(*z_copy(way, d - 1, half, False)).wait_recv()
        for way in range(2):
            if d < zh - 1 or (d == zh - 1 and way == half):
                send(*z_copy(way, d, half, True))
        if half == 1:
            to_twin((z + d) % nz)
            if 0 < d < zh:
                to_twin((z + nz - d) % nz)

    def y_copy(way, d, h, starting):
        slot = (ny - d) % ny if way == 0 else d
        later = ny - d - 1 if way == 0 else d + 1
        ts = pl.ds(0, tok)
        if d == yh - 1:
            ts = pl.ds(way * tb, tb)
        src, dst = norm_all.at[slot, h, ts], norm_all.at[later, h, ts]
        to = (y + 1) % ny if way == 0 else (y + ny - 1) % ny
        return src, dst, ys.at[way, d, h], yr.at[way, d, h], y_dev(to)

    def y_send(d, h):
        for way in range(2):
            send(*y_copy(way, d, h, True))

    def y_wait(d, h, ways=(0, 1)):
        for way in ways:
            remote(*y_copy(way, d - 1, h, False)).wait_recv()

    def norm(dst, query, inside, carried, scale):
        for b in range(2):
            ts = slice(b * tb, (b + 1) * tb)
            term = dot(query(ts), carried)
            mixture = inside(ts).astype(F32) + jnp.where(lo_ref[ts, :] < 0, term, 0.0)
            square_mean = jnp.mean(mixture * mixture, axis=-1, keepdims=True)
            gains = jnp.broadcast_to(scale[None, :], (tb, DH))
            dst[ts, :] = (mixture * lax.rsqrt(square_mean + 1e-06) * gains).astype(BF16)

    for h in range(heads):
        hs = slice(h * DH, (h + 1) * DH)
        wait_bytes(c_in.at[h, pl.ds(0, sl * (row - 1))], p3r.at[h])
        if h == 0:
            near_send(3)
        norm(norm_all.at[0, h], lambda ts: q_ref[ts, hs], lambda ts: within[h, ts, :], c_in[h], gain[hs])
        if h > 0:
            y_send(0, h)

    def project(rel, start=False):
        for b in range(2):
            ts = slice(b * tb, (b + 1) * tb)
            left = jnp.concatenate([norm_all[rel, h, ts, :] for h in range(heads)], axis=1)
            term = dot(left, wcol[rel])
            acc[ts, :] = term if start else acc[ts, :] + term

    def y_step(d, h):
        if d == 1 and h == 0:
            for way in range(2):
                for kind in range(4):
                    near_copy(way, kind).wait_recv()
                norm(
                    norm_all.at[ny - 1 if way == 0 else 1, 0], lambda ts: q_near[way, ts, :],
                    lambda ts: in_near[way, ts, :], c_near[way], g_near[way][0:DH])
        else:
            y_wait(d, h)
        y_send(d, h)

    loads[3].wait()
    project(0, True)
    wait_bytes(z_block(z, first_rel, yh), wyr)
    z_step(0, 0)
    z_step(0, 1)
    def side(e, core):
        return e + core * (ny - 2 * e)

    y_events = [(d, h) for d in range(1, yh) for h in range(heads)]
    z_events = [(d, half) for d in range(1, zh + 1) for half in range(2)]
    z_after = [min(max(m + 1, 2), len(y_events) - 2) for m in range(len(z_events))]
    for n, (d, h) in enumerate(y_events):
        y_step(d, h)
        for after, event in zip(z_after, z_events):
            if after == n:
                z_step(*event)
        if n == 2:
            for h2 in range(heads):
                wait_bytes(s_in.at[h2, others], p1s.at[h2])
                wait_bytes(s_in.at[h2, others], p3s.at[h2])
                for k in range(1, nz):
                    @pl.when(z + k < nz)
                    def _():
                        p2_copy(h2, k, z).wait_send()
            wait_bytes(z_block(z, first_rel, yh), wys)
        if n == len(y_events) // 2:
            early = len(sends)
        if n == len(y_events) - 2:
            for e in range(1, yh - 1):
                project(side(e, c))
        if n == len(y_events) - 1:
            project(side(yh - 1, c))
            wait_bytes(wcol.at[pl.ds(twin_rels, yh - 1)], wcr)
            wait_bytes(wcol.at[pl.ds(own_rels, yh - 1)], wcs)
            for copy in sends[:early]:
                copy.wait_send()
            for e in range(1, yh):
                project(side(e, 1 - c))
    for h in range(heads):
        hs = slice(h * DH, (h + 1) * DH)
        for way in range(2):
            ts = slice(way * tb, (way + 1) * tb)
            y_wait(yh, h, (way,))
            total = acc[ts, :] + dot(norm_all[yh, h, ts, :], wcol[yh, hs, :])
            if h < heads - 1:
                acc[ts, :] = total
            else:
                out_v[ts, :] = total.astype(BF16)
    for way in range(2):
        for kind in range(4):
            near_copy(way, kind).wait_send()
    for copy in sends[early:]:
        copy.wait_send()


def body(nz, row, ny, queries, key_vectors, value_vectors, doc_lengths, norm_gain, out_weight):
    tok, width = queries.shape
    heads = width // DH
    cols = out_weight.shape[1] // ny
    yh, zh = ny // 2, nz // 2
    sl = DH // row
    dma = pltpu.SemaphoreType.DMA
    any_spec = pl.BlockSpec(memory_space=pl.ANY)
    return pl.pallas_call(
        functools.partial(layer_kernel, nz, row, ny),
        name="layer",
        out_shape=pltpu.VMEM((tok, cols), BF16),
        in_specs=[any_spec] * 6,
        out_specs=pl.BlockSpec(memory_space=pltpu.VMEM),
        scratch_shapes=[
            pltpu.SMEM(doc_lengths.shape, jnp.int32),
            pltpu.VMEM((width,), F32),
            pltpu.VMEM((tok, width), BF16),
            pltpu.VMEM((tok, width), BF16),
            pltpu.VMEM((tok, width), BF16),
            pltpu.VMEM((heads, DH, DH), BF16),
            pltpu.VMEM((heads, row, sl, DH), BF16),
            pltpu.VMEM((heads, nz, sl, DH), BF16),
            pltpu.VMEM((heads, row, sl, DH), F32),
            pltpu.VMEM((heads, row, sl, DH), BF16),
            pltpu.VMEM((heads, DH, DH), BF16),
            pltpu.VMEM((tok, DH), jnp.int32),
            pltpu.VMEM((heads, tok, DH), F32),
            pltpu.VMEM((tok, DH), BF16),
            pltpu.VMEM((2, tok, DH), BF16),
            pltpu.VMEM((2, tok, DH), BF16),
            pltpu.VMEM((2, DH, DH), BF16),
            pltpu.VMEM((width,), F32),
            pltpu.VMEM((width,), F32),
            pltpu.VMEM((ny, heads, tok, DH), BF16),
            pltpu.VMEM((ny, width, cols), BF16),
            pltpu.VMEM((tok, cols), F32),
            dma((6,)),
            dma((heads,)), dma((heads,)),
            dma((heads, nz)), dma((heads, nz)),
            dma((heads,)), dma((heads,)),
            dma(()), dma(()),
            dma((2, 2, zh)), dma((2, 2, zh)),
            dma(()), dma(()),
            dma((2, yh, heads)), dma((2, yh, heads)),
            dma((2, 4)), dma((2, 4)),
            pltpu.SemaphoreType.REGULAR,
            pltpu.SemaphoreType.REGULAR((yh - 1,)),
        ],
        compiler_params=pltpu.CompilerParams(collective_id=0, has_side_effects=True),
    )(queries, key_vectors, value_vectors, doc_lengths, norm_gain, out_weight)


def solution(mesh, row=ROW):
    nz, ny = mesh.shape["seq"] // row, mesh.shape["head"]
    return jax.shard_map(
        functools.partial(body, nz, row, ny),
        mesh=mesh,
        in_specs=(
            P("seq", "head"),
            P("seq", "head"),
            P("seq", "head"),
            P(),
            P("head"),
            P("head", None),
        ),
        out_specs=P("seq", "head"),
        check_vma=False,
    )
```
